256 devices in a mesh: layer: 64 (over z_hi, y, x), space: 4 (over z_lo, core).
Axes of the slice: x: 4, y: 4, z: 8 (z_hi: 4, z_lo: 2; z = z_hi * 2 + z_lo), core: 2. Of those that a mesh axis runs over, the one named last changes fastest.
Arguments:
- input_field: float32 [16, 32, 256], P('space'), may hold values from -6 to 6
- weights: bfloat16 [128, 9, 256, 256], P('layer'), may hold values from -0.125 to 0.125
- cotangent: float32 [16, 32, 256], P('space'), may hold values from -6 to 6
Outputs:
- block_outputs: float32 [64, 16, 32, 256], P('layer', 'space')
- block_adjoints: float32 [64, 16, 32, 256], P('layer', 'space')
- weight_grad: bfloat16 [256, 128, 9, 256], P('space', 'layer')
The draws below stay inside these ranges and needn't reach their ends.
All inputs are finite; a program needn't handle non-finite values.
Results may differ from the reference program's by a relative error of at most 0.024.
Values may be sent and summed in bfloat16 or wider, within the bound.
A program may use at most 64 MiB of HBM per device.

```python
import jax
import jax.numpy as jnp
from jax import lax

CHANNELS = 256
LAY_DEV = 2
ROWS = 4
WIDTH = 32
ITERS = 2
BLOCKS = 64
LAYERS = 128
HEIGHT = 16
N_SPACE = 4


def block_scale(key, dims, split, smallest, top_value):
    factor_of, own = 1.0, jax.random.fold_in(key, 6)
    for dim, blocks in split:
        heights = jnp.exp(jax.random.uniform(jax.random.fold_in(own, dim), (blocks,), jnp.float32, smallest / len(split), top_value / len(split)))
        factor_of = factor_of * jnp.repeat(heights, dims[dim] // blocks).reshape([-1 if axis == dim else 1 for axis in range(len(dims))])
    return factor_of


def gaussian(key, dims, scale, reach, split=(), kind=jnp.bfloat16):
    factor_of = block_scale(key, dims, split, -0.22, 0.18) if split else 1.0
    values = jax.random.normal(key, dims, jnp.float32) * scale * factor_of
    return jnp.minimum(jnp.maximum(values, -reach), reach).astype(kind)


def setup_inputs(seed: int = 0) -> dict:
    streams_of = jax.random.split(jax.random.key(seed), 4)
    input_field = gaussian(streams_of[0], (HEIGHT, WIDTH, CHANNELS), 1.0, 6.0, ((0, 4),), jnp.float32)
    weights = gaussian(streams_of[1], (LAYERS, 9, CHANNELS, CHANNELS), (9 * CHANNELS) ** -0.5, 0.125, ((0, 64),))
    cotangent = gaussian(streams_of[2], (HEIGHT, WIDTH, CHANNELS), 1.0, 6.0, ((0, 4),), jnp.float32)
    return dict(input_field=input_field, weights=weights, cotangent=cotangent)


step_size = 0.125


def tap_stack(field, direction):
    height_here = field.shape[0]
    width_here = field.shape[1]
    padded = jnp.pad(field, ((1, 1), (1, 1), (0, 0)))
    return [padded[1 + direction * row_shift:1 + direction * row_shift + height_here, 1 + direction * col_shift:1 + direction * col_shift + width_here] for row_shift in (-1, 0, 1) for col_shift in (-1, 0, 1)]


def convolve(field_low, kernel):
    patches = jnp.concatenate(tap_stack(field_low, 1), axis=-1).reshape(-1, 9 * CHANNELS)
    mixed_sum = jnp.dot(patches, kernel.reshape(9 * CHANNELS, CHANNELS), preferred_element_type=jnp.float32)
    return mixed_sum.reshape(field_low.shape)


def transpose_conv(scaled, kernel):
    stacked = jnp.stack(tap_stack(scaled, -1), axis=2).astype(jnp.float32)
    return jnp.einsum("hwto,tio->hwi", stacked, kernel.astype(jnp.float32))


def forward_keep(operands):
    current, block_kernels = operands
    inputs_low = []
    slopes = []
    for layer_index in range(LAY_DEV):
        field_low = current.astype(jnp.bfloat16)
        squashed = jnp.tanh(convolve(field_low, block_kernels[layer_index]))
        inputs_low.append(field_low)
        slopes.append(1.0 - squashed * squashed)
        current = current + step_size * squashed
    return current, jnp.stack(inputs_low), jnp.stack(slopes)


def forward_only(operands):
    return forward_keep(operands)[0]


def backward_keep(operands):
    adjoint, block_kernels, slopes = operands
    scaled_list = [None] * LAY_DEV
    for layer_index in reversed(range(LAY_DEV)):
        scaled = (step_size * slopes[layer_index] * adjoint).astype(jnp.bfloat16)
        scaled_list[layer_index] = scaled
        adjoint = adjoint + transpose_conv(scaled, block_kernels[layer_index])
    return adjoint, jnp.stack(scaled_list)


def backward_only(operands):
    return backward_keep(operands)[0]


def block_gradient(operands):
    inputs_low, scaled = operands
    results = []
    for layer_index in range(LAY_DEV):
        patches = jnp.concatenate(tap_stack(inputs_low[layer_index], 1), axis=-1)
        patches = patches.reshape(N_SPACE, ROWS * WIDTH, 9 * CHANNELS).astype(jnp.float32)
        signal = scaled[layer_index].reshape(N_SPACE, ROWS * WIDTH, CHANNELS).astype(jnp.float32)
        partial_value = jnp.einsum("spo,spk->sok", signal, patches)
        partial_value = lax.optimization_barrier(partial_value.astype(jnp.bfloat16))
        results.append(jnp.sum(partial_value.astype(jnp.float32), axis=0).astype(jnp.bfloat16))
    return jnp.stack(results)


def reference(input_field, weights, cotangent):
    blocks = weights.reshape(BLOCKS, LAY_DEV, 9, CHANNELS, CHANNELS)
    begin_state = jnp.broadcast_to(input_field, (BLOCKS,) + input_field.shape).astype(jnp.float32)
    for sweep_index in range(ITERS):
        block_ends = lax.map(forward_only, (begin_state, blocks))
        block_jump = block_ends - begin_state
        begin_state = input_field + (jnp.cumsum(block_jump, axis=0) - block_jump)
    outputs, inputs_low, slopes = lax.map(forward_keep, (begin_state, blocks))
    finish = jnp.broadcast_to(cotangent, (BLOCKS,) + cotangent.shape).astype(jnp.float32)
    for sweep_index in range(ITERS):
        begins = lax.map(backward_only, (finish, blocks, slopes))
        back_jump = begins - finish
        running = jnp.cumsum(back_jump, axis=0)
        finish = cotangent + (running[-1:] - running)
    begins, scaled = lax.map(backward_keep, (finish, blocks, slopes))
    gradients = lax.map(block_gradient, (inputs_low, scaled))
    gradients = gradients.reshape(LAYERS, CHANNELS, 9, CHANNELS)
    weight_grad = jnp.transpose(gradients, (1, 0, 2, 3))
    return outputs, begins, weight_grad
```

```python
import jax
import jax.numpy as jnp
from jax import lax
from jax.sharding import PartitionSpec as P

ITERS = 2
RADIX = 4

step_size = 0.125


def conv(low, kernel3):
    return lax.conv_general_dilated(
        low[None],
        kernel3,
        (1, 1),
        ((1, 1), (1, 1)),
        dimension_numbers=("NHWC", "HWIO", "NHWC"),
        preferred_element_type=jnp.float32,
    )[0]


def conv_transposed(low, flipped3):
    return lax.conv_general_dilated(
        low[None],
        flipped3,
        (1, 1),
        ((1, 1), (1, 1)),
        dimension_numbers=("NHWC", "HWOI", "NHWC"),
        preferred_element_type=jnp.float32,
    )[0]


def forward_block(current, kernels):
    inputs_low = []
    slopes = []
    for kernel3 in kernels:
        low = current.astype(jnp.bfloat16)
        squashed = jnp.tanh(conv(low, kernel3))
        inputs_low.append(low)
        slopes.append(1.0 - squashed * squashed)
        current = current + step_size * squashed
    return current, inputs_low, slopes


def backward_block(adjoint, flipped, slopes):
    scaled_list = [None] * len(flipped)
    for index in reversed(range(len(flipped))):
        scaled = (step_size * slopes[index] * adjoint).astype(jnp.bfloat16)
        scaled_list[index] = scaled
        adjoint = adjoint + conv_transposed(scaled, flipped[index])
    return adjoint, scaled_list


def shifted_pairs(count, stride, shift):
    pairs = []
    for source in range(count):
        digit = (source // stride) % RADIX
        base = source - digit * stride
        pairs.append((source, base + ((digit + shift) % RADIX) * stride))
    return pairs


def exclusive_scan(value, reverse):
    count = lax.axis_size("layer")
    place = lax.axis_index("layer")
    total = jnp.zeros_like(value)
    stride = 1
    while stride < count:
        digit = (place // stride) % RADIX
        received = [
            lax.ppermute(value, "layer", shifted_pairs(count, stride, shift))
            for shift in range(1, RADIX)
        ]
        group = value
        for shift, part in zip(range(1, RADIX), received):
            earlier = shift > digit if reverse else shift <= digit
            total = total + jnp.where(earlier, part, jnp.zeros_like(part))
            group = group + part
        value = group
        stride *= RADIX
    return total


def gather_space(piece):
    count = lax.axis_size("space")
    place = lax.axis_index("space")
    rows = piece.shape[0]
    whole = jnp.zeros((count * rows,) + piece.shape[1:], piece.dtype)
    whole = lax.dynamic_update_slice_in_dim(whole, piece, place * rows, 0)
    for shift in range(1, count):
        part = lax.ppermute(
            piece, "space", [(i, (i + shift) % count) for i in range(count)]
        )
        source = (place + count - shift) % count
        whole = lax.dynamic_update_slice_in_dim(whole, part, source * rows, 0)
    return whole


def own_rows(whole, rows):
    return lax.dynamic_slice_in_dim(whole, lax.axis_index("space") * rows, rows, 0)


def on_device(input_field, weights, cotangent):
    rows = input_field.shape[0]
    channels = weights.shape[3]
    kernels = [w.reshape(3, 3, channels, channels) for w in weights]
    flipped = [k[::-1, ::-1] for k in kernels]
    full_input = gather_space(input_field)
    full_cotangent = gather_space(cotangent)

    begin_state = full_input
    for sweep_index in range(ITERS):
        block_end, _, _ = forward_block(begin_state, kernels)
        jump = own_rows(block_end - begin_state, rows)
        begin_state = gather_space(input_field + exclusive_scan(jump, False))
    outputs, inputs_low, slopes = forward_block(begin_state, kernels)

    finish = full_cotangent
    for sweep_index in range(ITERS):
        begins, _ = backward_block(finish, flipped, slopes)
        back = own_rows(begins - finish, rows)
        finish = gather_space(cotangent + exclusive_scan(back, True))
    begins, scaled_list = backward_block(finish, flipped, slopes)

    quarter = channels // lax.axis_size("space")
    first = lax.axis_index("space") * quarter
    height, width = inputs_low[0].shape[:2]
    pieces = []
    for low, scaled in zip(inputs_low, scaled_list):
        padded = jnp.pad(low, ((1, 1), (1, 1), (0, 0)))
        patches = jnp.concatenate(
            [
                padded[a : a + height, b : b + width]
                for a in range(3)
                for b in range(3)
            ],
            axis=-1,
        ).reshape(height * width, 9 * channels)
        signal = lax.dynamic_slice_in_dim(
            scaled.reshape(height * width, channels), first, quarter, 1
        )
        pieces.append(
            lax.dot_general(
                signal,
                patches,
                (((0,), (0,)), ((), ())),
                preferred_element_type=jnp.float32,
            ).reshape(quarter, 9, channels)
        )
    weight_grad = jnp.stack(pieces, axis=1).astype(jnp.bfloat16)
    return (own_rows(outputs, rows)[None], own_rows(begins, rows)[None], weight_grad)


def solution(mesh):
    placed = (P("space", None, None), P("layer", None, None, None), P("space", None, None))
    return jax.shard_map(
        on_device,
        mesh=mesh,
        in_specs=placed,
        out_specs=(
            P("layer", "space", None, None),
            P("layer", "space", None, None),
            P("space", "layer", None, None),
        ),
        check_vma=False,
    )
```

```python
import functools

import jax
import jax.numpy as jnp
from jax import lax
from jax.experimental import pallas as pl
from jax.experimental.pallas import tpu as pltpu
from jax.sharding import PartitionSpec as P

MESH = pl.DeviceIdType.MESH

ITERS = 2
RADIX = 4

step_size = 0.125


def conv(low, kernel3):
    return lax.conv_general_dilated(
        low[None],
        kernel3,
        (1, 1),
        ((1, 1), (1, 1)),
        dimension_numbers=("NHWC", "HWIO", "NHWC"),
        preferred_element_type=jnp.float32,
    )[0]


def conv_transposed(low, flipped3):
    return lax.conv_general_dilated(
        low[None],
        flipped3,
        (1, 1),
        ((1, 1), (1, 1)),
        dimension_numbers=("NHWC", "HWOI", "NHWC"),
        preferred_element_type=jnp.float32,
    )[0]


def forward_block(current, kernels):
    inputs_low = []
    slopes = []
    for kernel3 in kernels:
        low = current.astype(jnp.bfloat16)
        squashed = jnp.tanh(conv(low, kernel3))
        inputs_low.append(low)
        slopes.append(1.0 - squashed * squashed)
        current = current + step_size * squashed
    return current, inputs_low, slopes


def backward_block(adjoint, flipped, slopes):
    scaled_list = [None] * len(flipped)
    for index in reversed(range(len(flipped))):
        scaled = (step_size * slopes[index] * adjoint).astype(jnp.bfloat16)
        scaled_list[index] = scaled
        adjoint = adjoint + conv_transposed(scaled, flipped[index])
    return adjoint, scaled_list


def shifted_pairs(count, stride, shift):
    pairs = []
    for source in range(count):
        digit = (source // stride) % RADIX
        base = source - digit * stride
        pairs.append((source, base + ((digit + shift) % RADIX) * stride))
    return pairs


def exclusive_scan(value, reverse):
    count = lax.axis_size("layer")
    place = lax.axis_index("layer")
    total = jnp.zeros_like(value)
    stride = 1
    while stride < count:
        digit = (place // stride) % RADIX
        received = [
            lax.ppermute(value, "layer", shifted_pairs(count, stride, shift))
            for shift in range(1, RADIX)
        ]
        group = value
        for shift, part in zip(range(1, RADIX), received):
            earlier = shift > digit if reverse else shift <= digit
            total = total + jnp.where(earlier, part, jnp.zeros_like(part))
            group = group + part
        value = group
        stride *= RADIX
    return total


def scan_kernel(
    n_layer, n_space, reverse, value_ref, base_ref, out_ref,
    slots, gathered, group_buf, mine, send_sems, recv_sems, gsend, grecv,
):
    layer = lax.axis_index("layer")
    space = lax.axis_index("space")
    rows = value_ref.shape[0]
    strides = []
    stride = 1
    while stride < n_layer:
        strides.append(stride)
        stride *= RADIX

    partners = []
    for stride in strides:
        digit = (layer // stride) % RADIX
        base = layer - digit * stride
        for shift in range(1, RADIX):
            partners.append((base + ((digit + shift) % RADIX) * stride, space))
    for shift in range(1, n_space):
        partners.append((layer, (space + shift) % n_space))
    barrier = pltpu.get_barrier_semaphore()
    for partner in partners:
        pl.semaphore_signal(barrier, inc=1, device_id=partner, device_id_type=MESH)
    pl.semaphore_wait(barrier, len(partners))

    source = value_ref
    total = jnp.zeros(value_ref.shape, jnp.float32)
    for stage, stride in enumerate(strides):
        digit = (layer // stride) % RADIX
        base = layer - digit * stride
        copies = []
        for shift in range(1, RADIX):
            copy = pltpu.make_async_remote_copy(
                src_ref=source,
                dst_ref=slots.at[stage, shift - 1],
                send_sem=send_sems.at[stage, shift - 1],
                recv_sem=recv_sems.at[stage, shift - 1],
                device_id=(base + ((digit + shift) % RADIX) * stride, space),
                device_id_type=MESH,
            )
            copy.start()
            copies.append(copy)
        for copy in copies:
            copy.wait()
        group = source[...]
        for shift in range(1, RADIX):
            part = slots[stage, shift - 1]
            earlier = shift > digit if reverse else shift <= digit
            total = total + jnp.where(earlier, part, jnp.zeros_like(part))
            group = group + part
        if stage + 1 < len(strides):
            group_buf[stage] = group
            source = group_buf.at[stage]

    mine[...] = base_ref[...] + total
    copies = []
    for shift in range(1, n_space):
        copy = pltpu.make_async_remote_copy(
            src_ref=mine,
            dst_ref=gathered.at[shift - 1],
            send_sem=gsend.at[shift - 1],
            recv_sem=grecv.at[shift - 1],
            device_id=(layer, (space + shift) % n_space),
            device_id_type=MESH,
        )
        copy.start()
        copies.append(copy)
    out_ref[pl.ds(space * rows, rows)] = mine[...]
    for copy in copies:
        copy.wait()
    for shift in range(1, n_space):
        origin = (space + n_space - shift) % n_space
        out_ref[pl.ds(origin * rows, rows)] = gathered[shift - 1]


def scan_and_gather(value, base, reverse, collective_id):
    n_layer = lax.axis_size("layer")
    n_space = lax.axis_size("space")
    stages = 0
    while RADIX ** stages < n_layer:
        stages += 1
    assert RADIX ** stages == n_layer
    rows, width, channels = value.shape
    piece = (rows, width, channels)
    return pl.pallas_call(
        functools.partial(scan_kernel, n_layer, n_space, reverse),
        out_shape=jax.ShapeDtypeStruct((n_space * rows, width, channels), jnp.float32),
        in_specs=[pl.BlockSpec(memory_space=pltpu.VMEM)] * 2,
        out_specs=pl.BlockSpec(memory_space=pltpu.VMEM),
        scratch_shapes=[
            pltpu.VMEM((stages, RADIX - 1) + piece, jnp.float32),
            pltpu.VMEM((n_space - 1,) + piece, jnp.float32),
            pltpu.VMEM((max(stages - 1, 1),) + piece, jnp.float32),
            pltpu.VMEM(piece, jnp.float32),
            pltpu.SemaphoreType.DMA((stages, RADIX - 1)),
            pltpu.SemaphoreType.DMA((stages, RADIX - 1)),
            pltpu.SemaphoreType.DMA((n_space - 1,)),
            pltpu.SemaphoreType.DMA((n_space - 1,)),
        ],
        compiler_params=pltpu.CompilerParams(
            collective_id=collective_id, has_side_effects=True
        ),
    )(value, base)


def gather_space(piece):
    count = lax.axis_size("space")
    place = lax.axis_index("space")
    rows = piece.shape[0]
    whole = jnp.zeros((count * rows,) + piece.shape[1:], piece.dtype)
    whole = lax.dynamic_update_slice_in_dim(whole, piece, place * rows, 0)
    for shift in range(1, count):
        part = lax.ppermute(
            piece, "space", [(i, (i + shift) % count) for i in range(count)]
        )
        source = (place + count - shift) % count
        whole = lax.dynamic_update_slice_in_dim(whole, part, source * rows, 0)
    return whole


def own_rows(whole, rows):
    return lax.dynamic_slice_in_dim(whole, lax.axis_index("space") * rows, rows, 0)


def on_device(input_field, weights, cotangent):
    rows = input_field.shape[0]
    channels = weights.shape[3]
    kernels = [w.reshape(3, 3, channels, channels) for w in weights]
    flipped = [k[::-1, ::-1] for k in kernels]
    full_input = gather_space(input_field)
    full_cotangent = gather_space(cotangent)

    begin_state = full_input
    for sweep_index in range(ITERS):
        block_end, _, _ = forward_block(begin_state, kernels)
        jump = own_rows(block_end - begin_state, rows)
        begin_state = scan_and_gather(jump, input_field, False, sweep_index)
    outputs, inputs_low, slopes = forward_block(begin_state, kernels)

    finish = full_cotangent
    for sweep_index in range(ITERS):
        begins, _ = backward_block(finish, flipped, slopes)
        back = own_rows(begins - finish, rows)
        finish = scan_and_gather(back, cotangent, True, ITERS + sweep_index)
    begins, scaled_list = backward_block(finish, flipped, slopes)

    quarter = channels // lax.axis_size("space")
    first = lax.axis_index("space") * quarter
    height, width = inputs_low[0].shape[:2]
    pieces = []
    for low, scaled in zip(inputs_low, scaled_list):
        padded = jnp.pad(low, ((1, 1), (1, 1), (0, 0)))
        patches = jnp.concatenate(
            [
                padded[a : a + height, b : b + width]
                for a in range(3)
                for b in range(3)
            ],
            axis=-1,
        ).reshape(height * width, 9 * channels)
        signal = lax.dynamic_slice_in_dim(
            scaled.reshape(height * width, channels), first, quarter, 1
        )
        pieces.append(
            lax.dot_general(
                signal,
                patches,
                (((0,), (0,)), ((), ())),
                preferred_element_type=jnp.float32,
            ).reshape(quarter, 9, channels)
        )
    weight_grad = jnp.stack(pieces, axis=1).astype(jnp.bfloat16)
    return (own_rows(outputs, rows)[None], own_rows(begins, rows)[None], weight_grad)


def solution(mesh):
    placed = (P("space", None, None), P("layer", None, None, None), P("space", None, None))
    return jax.shard_map(
        on_device,
        mesh=mesh,
        in_specs=placed,
        out_specs=(
            P("layer", "space", None, None),
            P("layer", "space", None, None),
            P("space", "layer", None, None),
        ),
        check_vma=False,
    )
```

```python
import functools

import jax
import jax.numpy as jnp
from jax import lax
from jax.experimental import pallas as pl
from jax.experimental.pallas import tpu as pltpu
from jax.sharding import PartitionSpec as P

MESH = pl.DeviceIdType.MESH

ITERS = 2
RADIX = 4

step_size = 0.125


def conv(low, kernel3):
    return lax.conv_general_dilated(
        low[None],
        kernel3,
        (1, 1),
        ((1, 1), (1, 1)),
        dimension_numbers=("NHWC", "HWIO", "NHWC"),
        preferred_element_type=jnp.float32,
    )[0]


def conv_transposed(low, flipped3):
    return lax.conv_general_dilated(
        low[None],
        flipped3,
        (1, 1),
        ((1, 1), (1, 1)),
        dimension_numbers=("NHWC", "HWOI", "NHWC"),
        preferred_element_type=jnp.float32,
    )[0]


def forward_block(current, kernels):
    inputs_low = []
    slopes = []
    for kernel3 in kernels:
        low = current.astype(jnp.bfloat16)
        squashed = jnp.tanh(conv(low, kernel3))
        inputs_low.append(low)
        slopes.append(1.0 - squashed * squashed)
        current = current + step_size * squashed
    return current, inputs_low, slopes


def backward_block(adjoint, flipped, slopes):
    scaled_list = [None] * len(flipped)
    for index in reversed(range(len(flipped))):
        scaled = (step_size * slopes[index] * adjoint).astype(jnp.bfloat16)
        scaled_list[index] = scaled
        adjoint = adjoint + conv_transposed(scaled, flipped[index])
    return adjoint, scaled_list


def shifted_pairs(count, stride, shift):
    pairs = []
    for source in range(count):
        digit = (source // stride) % RADIX
        base = source - digit * stride
        pairs.append((source, base + ((digit + shift) % RADIX) * stride))
    return pairs


def exclusive_scan(value, reverse):
    count = lax.axis_size("layer")
    place = lax.axis_index("layer")
    total = jnp.zeros_like(value)
    stride = 1
    while stride < count:
        digit = (place // stride) % RADIX
        received = [
            lax.ppermute(value, "layer", shifted_pairs(count, stride, shift))
            for shift in range(1, RADIX)
        ]
        group = value
        for shift, part in zip(range(1, RADIX), received):
            earlier = shift > digit if reverse else shift <= digit
            total = total + jnp.where(earlier, part, jnp.zeros_like(part))
            group = group + part
        value = group
        stride *= RADIX
    return total


def scan_kernel(
    n_layer, n_space, reverse, value_ref, base_ref, out_ref,
    slots, gathered, group_buf, mine, total, send_sems, recv_sems, gsend, grecv,
):
    layer = lax.axis_index("layer")
    space = lax.axis_index("space")
    rows = value_ref.shape[0]
    strides = []
    stride = 1
    while stride < n_layer:
        strides.append(stride)
        stride *= RADIX

    partners = []
    for stride in strides:
        digit = (layer // stride) % RADIX
        base = layer - digit * stride
        for shift in range(1, RADIX):
            partners.append((base + ((digit + shift) % RADIX) * stride, space))
    for shift in range(1, n_space):
        partners.append((layer, (space + shift) % n_space))
    barrier = pltpu.get_barrier_semaphore()
    for partner in partners:
        pl.semaphore_signal(barrier, inc=1, device_id=partner, device_id_type=MESH)
    pl.semaphore_wait(barrier, len(partners))

    total[...] = jnp.zeros(total.shape, jnp.float32)
    source = value_ref
    for stage, stride in enumerate(strides):
        last = stage + 1 == len(strides)
        digit = (layer // stride) % RADIX
        base = layer - digit * stride
        copies = []
        for shift in range(1, RADIX):
            copy = pltpu.make_async_remote_copy(
                src_ref=source,
                dst_ref=slots.at[stage, shift - 1],
                send_sem=send_sems.at[stage, shift - 1],
                recv_sem=recv_sems.at[stage, shift - 1],
                device_id=(base + ((digit + shift) % RADIX) * stride, space),
                device_id_type=MESH,
            )
            wraps = digit + shift >= RADIX
            sends = (wraps if reverse else jnp.logical_not(wraps)) if last else None
            gets = (shift > digit if reverse else shift <= digit) if last else None
            copies.append((copy, sends, gets))
            if last:
                pl.when(sends)(copy.start)
            else:
                copy.start()
        for shift, (copy, sends, gets) in zip(range(1, RADIX), copies):
            if last:
                pl.when(sends)(copy.wait_send)
                pl.when(gets)(copy.wait_recv)
            else:
                copy.wait()
        group = source[...].astype(jnp.float32)
        for shift in range(1, RADIX):
            earlier = shift > digit if reverse else shift <= digit

            @pl.when(earlier)
            def _():
                total[...] += slots[stage, shift - 1].astype(jnp.float32)

            if not last:
                group = group + slots[stage, shift - 1].astype(jnp.float32)
        if not last:
            group_buf[stage] = group.astype(group_buf.dtype)
            source = group_buf.at[stage]

    mine[...] = base_ref[...] + total[...]
    copies = []
    for shift in range(1, n_space):
        copy = pltpu.make_async_remote_copy(
            src_ref=mine,
            dst_ref=gathered.at[shift - 1],
            send_sem=gsend.at[shift - 1],
            recv_sem=grecv.at[shift - 1],
            device_id=(layer, (space + shift) % n_space),
            device_id_type=MESH,
        )
        copy.start()
        copies.append(copy)
    out_ref[pl.ds(space * rows, rows)] = mine[...]
    for copy in copies:
        copy.wait()
    for shift in range(1, n_space):
        origin = (space + n_space - shift) % n_space
        out_ref[pl.ds(origin * rows, rows)] = gathered[shift - 1]


def scan_and_gather(value, base, reverse, collective_id):
    n_layer = lax.axis_size("layer")
    n_space = lax.axis_size("space")
    stages = 0
    while RADIX ** stages < n_layer:
        stages += 1
    assert RADIX ** stages == n_layer
    rows, width, channels = value.shape
    piece = (rows, width, channels)
    link = jnp.bfloat16
    return pl.pallas_call(
        functools.partial(scan_kernel, n_layer, n_space, reverse),
        out_shape=jax.ShapeDtypeStruct((n_space * rows, width, channels), jnp.float32),
        in_specs=[pl.BlockSpec(memory_space=pltpu.VMEM)] * 2,
        out_specs=pl.BlockSpec(memory_space=pltpu.VMEM),
        scratch_shapes=[
            pltpu.VMEM((stages, RADIX - 1) + piece, link),
            pltpu.VMEM((n_space - 1,) + piece, jnp.float32),
            pltpu.VMEM((max(stages - 1, 1),) + piece, link),
            pltpu.VMEM(piece, jnp.float32),
            pltpu.VMEM(piece, jnp.float32),
            pltpu.SemaphoreType.DMA((stages, RADIX - 1)),
            pltpu.SemaphoreType.DMA((stages, RADIX - 1)),
            pltpu.SemaphoreType.DMA((n_space - 1,)),
            pltpu.SemaphoreType.DMA((n_space - 1,)),
        ],
        compiler_params=pltpu.CompilerParams(
            collective_id=collective_id,
            has_side_effects=True,
            vmem_limit_bytes=8 * 1024 * 1024,
        ),
    )(value.astype(link), base)


def gather_space(piece):
    count = lax.axis_size("space")
    place = lax.axis_index("space")
    rows = piece.shape[0]
    whole = jnp.zeros((count * rows,) + piece.shape[1:], piece.dtype)
    whole = lax.dynamic_update_slice_in_dim(whole, piece, place * rows, 0)
    for shift in range(1, count):
        part = lax.ppermute(
            piece, "space", [(i, (i + shift) % count) for i in range(count)]
        )
        source = (place + count - shift) % count
        whole = lax.dynamic_update_slice_in_dim(whole, part, source * rows, 0)
    return whole


def own_rows(whole, rows):
    return lax.dynamic_slice_in_dim(whole, lax.axis_index("space") * rows, rows, 0)


def on_device(input_field, weights, cotangent):
    rows = input_field.shape[0]
    channels = weights.shape[3]
    kernels = [w.reshape(3, 3, channels, channels) for w in weights]
    flipped = [k[::-1, ::-1] for k in kernels]
    full_input = gather_space(input_field)
    full_cotangent = gather_space(cotangent)

    begin_state = full_input
    for sweep_index in range(ITERS):
        block_end, _, _ = forward_block(begin_state, kernels)
        jump = own_rows(block_end - begin_state, rows)
        begin_state = scan_and_gather(jump, input_field, False, sweep_index)
    outputs, inputs_low, slopes = forward_block(begin_state, kernels)

    finish = full_cotangent
    for sweep_index in range(ITERS):
        begins, _ = backward_block(finish, flipped, slopes)
        back = own_rows(begins - finish, rows)
        finish = scan_and_gather(back, cotangent, True, ITERS + sweep_index)
    begins, scaled_list = backward_block(finish, flipped, slopes)

    quarter = channels // lax.axis_size("space")
    first = lax.axis_index("space") * quarter
    height, width = inputs_low[0].shape[:2]
    pieces = []
    for low, scaled in zip(inputs_low, scaled_list):
        padded = jnp.pad(low, ((1, 1), (1, 1), (0, 0)))
        patches = jnp.concatenate(
            [
                padded[a : a + height, b : b + width]
                for a in range(3)
                for b in range(3)
            ],
            axis=-1,
        ).reshape(height * width, 9 * channels)
        signal = lax.dynamic_slice_in_dim(
            scaled.reshape(height * width, channels), first, quarter, 1
        )
        pieces.append(
            lax.dot_general(
                signal,
                patches,
                (((0,), (0,)), ((), ())),
                preferred_element_type=jnp.float32,
            ).reshape(quarter, 9, channels)
        )
    weight_grad = jnp.stack(pieces, axis=1).astype(jnp.bfloat16)
    return (own_rows(outputs, rows)[None], own_rows(begins, rows)[None], weight_grad)


def solution(mesh):
    placed = (P("space", None, None), P("layer", None, None, None), P("space", None, None))
    return jax.shard_map(
        on_device,
        mesh=mesh,
        in_specs=placed,
        out_specs=(
            P("layer", "space", None, None),
            P("layer", "space", None, None),
            P("space", "layer", None, None),
        ),
        check_vma=False,
    )
```

```python
import functools

import jax
import jax.numpy as jnp
from jax import lax
from jax.experimental import pallas as pl
from jax.experimental.pallas import tpu as pltpu
from jax.sharding import PartitionSpec as P

MESH = pl.DeviceIdType.MESH

ITERS = 2
RADIX = 4

step_size = 0.125


CHUNK = 4


def column_chunks(low):
    height, width, channels = low.shape
    padded = jnp.pad(low, ((0, 0), (1, 1), (0, 0)))
    return jnp.stack(
        [padded[:, c : c + CHUNK + 2] for c in range(0, width, CHUNK)], axis=1
    )


def chunked_conv(low, kernel3, spec):
    height, width, channels = low.shape
    out = lax.conv_general_dilated(
        column_chunks(low),
        kernel3,
        (1, 1),
        ((1, 1), (0, 0)),
        dimension_numbers=("HNWC", spec, "HNWC"),
        preferred_element_type=jnp.float32,
    )
    return out.reshape(height, width, kernel3.shape[3] if spec == "HWIO" else kernel3.shape[2])


def conv(low, kernel3):
    return chunked_conv(low, kernel3, "HWIO")


def conv_transposed(low, flipped3):
    return chunked_conv(low, flipped3, "HWOI")


def kernel_gradient(low, signal):
    return lax.conv_general_dilated(
        low[None],
        signal[None],
        (1, 1),
        ((1, 1), (1, 1)),
        dimension_numbers=("CHWN", "IHWO", "NHWC"),
        preferred_element_type=jnp.float32,
    )


def forward_block(current, kernels):
    inputs_low = []
    slopes = []
    for kernel3 in kernels:
        low = current.astype(jnp.bfloat16)
        squashed = jnp.tanh(conv(low, kernel3))
        inputs_low.append(low)
        slopes.append(1.0 - squashed * squashed)
        current = current + step_size * squashed
    return current, inputs_low, slopes


def backward_block(adjoint, flipped, slopes):
    scaled_list = [None] * len(flipped)
    for index in reversed(range(len(flipped))):
        scaled = (step_size * slopes[index] * adjoint).astype(jnp.bfloat16)
        scaled_list[index] = scaled
        adjoint = adjoint + conv_transposed(scaled, flipped[index])
    return adjoint, scaled_list


def shifted_pairs(count, stride, shift):
    pairs = []
    for source in range(count):
        digit = (source // stride) % RADIX
        base = source - digit * stride
        pairs.append((source, base + ((digit + shift) % RADIX) * stride))
    return pairs


def exclusive_scan(value, reverse):
    count = lax.axis_size("layer")
    place = lax.axis_index("layer")
    total = jnp.zeros_like(value)
    stride = 1
    while stride < count:
        digit = (place // stride) % RADIX
        received = [
            lax.ppermute(value, "layer", shifted_pairs(count, stride, shift))
            for shift in range(1, RADIX)
        ]
        group = value
        for shift, part in zip(range(1, RADIX), received):
            earlier = shift > digit if reverse else shift <= digit
            total = total + jnp.where(earlier, part, jnp.zeros_like(part))
            group = group + part
        value = group
        stride *= RADIX
    return total


def scan_kernel(
    n_layer, n_space, reverse, value_ref, base_ref, out_ref,
    slots, gathered, group_buf, mine, total, send_sems, recv_sems, gsend, grecv,
):
    layer = lax.axis_index("layer")
    space = lax.axis_index("space")
    rows = value_ref.shape[0]
    strides = []
    stride = 1
    while stride < n_layer:
        strides.append(stride)
        stride *= RADIX

    partners = []
    for stride in strides:
        digit = (layer // stride) % RADIX
        base = layer - digit * stride
        for shift in range(1, RADIX):
            partners.append((base + ((digit + shift) % RADIX) * stride, space))
    for shift in range(1, n_space):
        partners.append((layer, (space + shift) % n_space))
    barrier = pltpu.get_barrier_semaphore()
    for partner in partners:
        pl.semaphore_signal(barrier, inc=1, device_id=partner, device_id_type=MESH)
    pl.semaphore_wait(barrier, len(partners))

    total[...] = jnp.zeros(total.shape, jnp.float32)
    source = value_ref
    for stage, stride in enumerate(strides):
        last = stage + 1 == len(strides)
        digit = (layer // stride) % RADIX
        base = layer - digit * stride
        copies = []
        for shift in range(1, RADIX):
            copy = pltpu.make_async_remote_copy(
                src_ref=source,
                dst_ref=slots.at[stage, shift - 1],
                send_sem=send_sems.at[stage, shift - 1],
                recv_sem=recv_sems.at[stage, shift - 1],
                device_id=(base + ((digit + shift) % RADIX) * stride, space),
                device_id_type=MESH,
            )
            wraps = digit + shift >= RADIX
            sends = (wraps if reverse else jnp.logical_not(wraps)) if last else None
            gets = (shift > digit if reverse else shift <= digit) if last else None
            copies.append((copy, sends, gets))
            if last:
                pl.when(sends)(copy.start)
            else:
                copy.start()
        for shift, (copy, sends, gets) in zip(range(1, RADIX), copies):
            if last:
                pl.when(sends)(copy.wait_send)
                pl.when(gets)(copy.wait_recv)
            else:
                copy.wait()
        group = source[...].astype(jnp.float32)
        for shift in range(1, RADIX):
            earlier = shift > digit if reverse else shift <= digit

            @pl.when(earlier)
            def _():
                total[...] += slots[stage, shift - 1].astype(jnp.float32)

            if not last:
                group = group + slots[stage, shift - 1].astype(jnp.float32)
        if not last:
            group_buf[stage] = group.astype(group_buf.dtype)
            source = group_buf.at[stage]

    mine[...] = total[...].astype(mine.dtype)
    copies = []
    for shift in range(1, n_space):
        copy = pltpu.make_async_remote_copy(
            src_ref=mine,
            dst_ref=gathered.at[shift - 1],
            send_sem=gsend.at[shift - 1],
            recv_sem=grecv.at[shift - 1],
            device_id=(layer, (space + shift) % n_space),
            device_id_type=MESH,
        )
        copy.start()
        copies.append(copy)
    here = pl.ds(space * rows, rows)
    out_ref[here] = base_ref[here] + total[...]
    for copy in copies:
        copy.wait()
    for shift in range(1, n_space):
        there = pl.ds(((space + n_space - shift) % n_space) * rows, rows)
        out_ref[there] = base_ref[there] + gathered[shift - 1].astype(jnp.float32)


def scan_and_gather(value, base, reverse, collective_id):
    n_layer = lax.axis_size("layer")
    n_space = lax.axis_size("space")
    stages = 0
    while RADIX ** stages < n_layer:
        stages += 1
    assert RADIX ** stages == n_layer
    rows, width, channels = value.shape
    piece = (rows, width, channels)
    link = jnp.bfloat16
    return pl.pallas_call(
        functools.partial(scan_kernel, n_layer, n_space, reverse),
        out_shape=jax.ShapeDtypeStruct((n_space * rows, width, channels), jnp.float32),
        in_specs=[pl.BlockSpec(memory_space=pltpu.VMEM)] * 2,
        out_specs=pl.BlockSpec(memory_space=pltpu.VMEM),
        scratch_shapes=[
            pltpu.VMEM((stages, RADIX - 1) + piece, link),
            pltpu.VMEM((n_space - 1,) + piece, link),
            pltpu.VMEM((max(stages - 1, 1),) + piece, link),
            pltpu.VMEM(piece, link),
            pltpu.VMEM(piece, jnp.float32),
            pltpu.SemaphoreType.DMA((stages, RADIX - 1)),
            pltpu.SemaphoreType.DMA((stages, RADIX - 1)),
            pltpu.SemaphoreType.DMA((n_space - 1,)),
            pltpu.SemaphoreType.DMA((n_space - 1,)),
        ],
        compiler_params=pltpu.CompilerParams(
            collective_id=collective_id,
            has_side_effects=True,
            vmem_limit_bytes=8 * 1024 * 1024,
        ),
    )(value.astype(link), base)


def gather_space(piece):
    count = lax.axis_size("space")
    place = lax.axis_index("space")
    rows = piece.shape[0]
    whole = jnp.zeros((count * rows,) + piece.shape[1:], piece.dtype)
    whole = lax.dynamic_update_slice_in_dim(whole, piece, place * rows, 0)
    for shift in range(1, count):
        part = lax.ppermute(
            piece, "space", [(i, (i + shift) % count) for i in range(count)]
        )
        source = (place + count - shift) % count
        whole = lax.dynamic_update_slice_in_dim(whole, part, source * rows, 0)
    return whole


def own_rows(whole, rows):
    return lax.dynamic_slice_in_dim(whole, lax.axis_index("space") * rows, rows, 0)


def on_device(input_field, weights, cotangent):
    rows = input_field.shape[0]
    channels = weights.shape[3]
    kernels = [w.reshape(3, 3, channels, channels) for w in weights]
    flipped = [k[::-1, ::-1] for k in kernels]
    full_input = gather_space(input_field)
    full_cotangent = gather_space(cotangent)

    begin_state = full_input
    for sweep_index in range(ITERS):
        block_end, _, _ = forward_block(begin_state, kernels)
        jump = own_rows(block_end - begin_state, rows)
        begin_state = scan_and_gather(jump, full_input, False, sweep_index)
    outputs, inputs_low, slopes = forward_block(begin_state, kernels)

    finish = full_cotangent
    for sweep_index in range(ITERS):
        begins, _ = backward_block(finish, flipped, slopes)
        back = own_rows(begins - finish, rows)
        finish = scan_and_gather(back, full_cotangent, True, ITERS + sweep_index)
    begins, scaled_list = backward_block(finish, flipped, slopes)

    quarter = channels // lax.axis_size("space")
    first = lax.axis_index("space") * quarter
    pieces = []
    for low, scaled in zip(inputs_low, scaled_list):
        signal = lax.dynamic_slice_in_dim(scaled, first, quarter, 2)
        grad = kernel_gradient(low, signal)
        pieces.append(jnp.transpose(grad, (3, 1, 2, 0)).reshape(quarter, 9, channels))
    weight_grad = jnp.stack(pieces, axis=1).astype(jnp.bfloat16)
    return (own_rows(outputs, rows)[None], own_rows(begins, rows)[None], weight_grad)


def solution(mesh):
    placed = (P("space", None, None), P("layer", None, None, None), P("space", None, None))
    return jax.shard_map(
        on_device,
        mesh=mesh,
        in_specs=placed,
        out_specs=(
            P("layer", "space", None, None),
            P("layer", "space", None, None),
            P("space", "layer", None, None),
        ),
        check_vma=False,
    )
```

```python
import functools

import jax
import jax.numpy as jnp
from jax import lax
from jax.experimental import pallas as pl
from jax.experimental.pallas import tpu as pltpu
from jax.sharding import PartitionSpec as P

MESH = pl.DeviceIdType.MESH

ITERS = 2
RADIX = 4

step_size = 0.125


CHUNK = 4


def column_chunks(low):
    height, width, channels = low.shape
    padded = jnp.pad(low, ((0, 0), (1, 1), (0, 0)))
    return jnp.stack(
        [padded[:, c : c + CHUNK + 2] for c in range(0, width, CHUNK)], axis=1
    )


def chunked_conv(low, kernel3, spec):
    height, width, channels = low.shape
    out = lax.conv_general_dilated(
        column_chunks(low),
        kernel3,
        (1, 1),
        ((1, 1), (0, 0)),
        dimension_numbers=("HNWC", spec, "HNWC"),
        preferred_element_type=jnp.float32,
    )
    return out.reshape(height, width, kernel3.shape[3] if spec == "HWIO" else kernel3.shape[2])


def conv(low, kernel3):
    return chunked_conv(low, kernel3, "HWIO")


def conv_transposed(low, flipped3):
    return chunked_conv(low, flipped3, "HWOI")


def kernel_gradient(low, signal):
    return lax.conv_general_dilated(
        low[None],
        signal[None],
        (1, 1),
        ((1, 1), (1, 1)),
        dimension_numbers=("CHWN", "IHWO", "NHWC"),
        preferred_element_type=jnp.float32,
    )


def forward_block(current, kernels):
    inputs_low = []
    slopes = []
    for kernel3 in kernels:
        low = current.astype(jnp.bfloat16)
        squashed = jnp.tanh(conv(low, kernel3))
        inputs_low.append(low)
        slopes.append(1.0 - squashed * squashed)
        current = current + step_size * squashed
    return current, inputs_low, slopes


def backward_block(adjoint, flipped, slopes):
    scaled_list = [None] * len(flipped)
    for index in reversed(range(len(flipped))):
        scaled = (step_size * slopes[index] * adjoint).astype(jnp.bfloat16)
        scaled_list[index] = scaled
        adjoint = adjoint + conv_transposed(scaled, flipped[index])
    return adjoint, scaled_list


def shifted_pairs(count, stride, shift):
    pairs = []
    for source in range(count):
        digit = (source // stride) % RADIX
        base = source - digit * stride
        pairs.append((source, base + ((digit + shift) % RADIX) * stride))
    return pairs


def exclusive_scan(value, reverse):
    count = lax.axis_size("layer")
    place = lax.axis_index("layer")
    total = jnp.zeros_like(value)
    stride = 1
    while stride < count:
        digit = (place // stride) % RADIX
        received = [
            lax.ppermute(value, "layer", shifted_pairs(count, stride, shift))
            for shift in range(1, RADIX)
        ]
        group = value
        for shift, part in zip(range(1, RADIX), received):
            earlier = shift > digit if reverse else shift <= digit
            total = total + jnp.where(earlier, part, jnp.zeros_like(part))
            group = group + part
        value = group
        stride *= RADIX
    return total


def scan_kernel(
    n_layer, n_space, reverse, value_ref, base_ref, out_ref,
    slots, gathered, group_buf, mine, total, send_sems, recv_sems, gsend, grecv,
):
    layer = lax.axis_index("layer")
    space = lax.axis_index("space")
    rows = value_ref.shape[0]
    strides = []
    stride = 1
    while stride < n_layer:
        strides.append(stride)
        stride *= RADIX

    partners = []
    for stride in strides:
        digit = (layer // stride) % RADIX
        base = layer - digit * stride
        for shift in range(1, RADIX):
            partners.append((base + ((digit + shift) % RADIX) * stride, space))
    for shift in range(1, n_space):
        partners.append((layer, (space + shift) % n_space))
    barrier = pltpu.get_barrier_semaphore()
    for partner in partners:
        pl.semaphore_signal(barrier, inc=1, device_id=partner, device_id_type=MESH)
    pl.semaphore_wait(barrier, len(partners))

    total[...] = jnp.zeros(total.shape, jnp.float32)
    pending = []
    source = value_ref
    for stage, stride in enumerate(strides):
        last = stage + 1 == len(strides)
        digit = (layer // stride) % RADIX
        base = layer - digit * stride
        copies = []
        for shift in range(1, RADIX):
            copy = pltpu.make_async_remote_copy(
                src_ref=source,
                dst_ref=slots.at[stage, shift - 1],
                send_sem=send_sems.at[stage, shift - 1],
                recv_sem=recv_sems.at[stage, shift - 1],
                device_id=(base + ((digit + shift) % RADIX) * stride, space),
                device_id_type=MESH,
            )
            wraps = digit + shift >= RADIX
            sends = (wraps if reverse else jnp.logical_not(wraps)) if last else None
            gets = (shift > digit if reverse else shift <= digit) if last else None
            copies.append((copy, sends, gets))
            if last:
                pl.when(sends)(copy.start)
            else:
                copy.start()
        for shift, (copy, sends, gets) in zip(range(1, RADIX), copies):
            if last:
                pl.when(gets)(copy.wait_recv)
            else:
                copy.wait_recv()
            pending.append((copy, sends))
        group = source[...].astype(jnp.float32)
        for shift in range(1, RADIX):
            earlier = shift > digit if reverse else shift <= digit

            @pl.when(earlier)
            def _():
                total[...] += slots[stage, shift - 1].astype(jnp.float32)

            if not last:
                group = group + slots[stage, shift - 1].astype(jnp.float32)
        if not last:
            group_buf[stage] = group.astype(group_buf.dtype)
            source = group_buf.at[stage]

    mine[...] = total[...].astype(mine.dtype)
    copies = []
    for shift in range(1, n_space):
        copy = pltpu.make_async_remote_copy(
            src_ref=mine,
            dst_ref=gathered.at[shift - 1],
            send_sem=gsend.at[shift - 1],
            recv_sem=grecv.at[shift - 1],
            device_id=(layer, (space + shift) % n_space),
            device_id_type=MESH,
        )
        copy.start()
        copies.append(copy)
    here = pl.ds(space * rows, rows)
    out_ref[here] = base_ref[here] + total[...]
    for copy in copies:
        copy.wait_recv()
    for shift in range(1, n_space):
        there = pl.ds(((space + n_space - shift) % n_space) * rows, rows)
        out_ref[there] = base_ref[there] + gathered[shift - 1].astype(jnp.float32)
    for copy, sends in pending:
        if sends is None:
            copy.wait_send()
        else:
            pl.when(sends)(copy.wait_send)
    for copy in copies:
        copy.wait_send()


def scan_and_gather(value, base, reverse, collective_id):
    n_layer = lax.axis_size("layer")
    n_space = lax.axis_size("space")
    stages = 0
    while RADIX ** stages < n_layer:
        stages += 1
    assert RADIX ** stages == n_layer
    rows, width, channels = value.shape
    piece = (rows, width, channels)
    link = jnp.bfloat16
    return pl.pallas_call(
        functools.partial(scan_kernel, n_layer, n_space, reverse),
        out_shape=jax.ShapeDtypeStruct((n_space * rows, width, channels), jnp.float32),
        in_specs=[pl.BlockSpec(memory_space=pltpu.VMEM)] * 2,
        out_specs=pl.BlockSpec(memory_space=pltpu.VMEM),
        scratch_shapes=[
            pltpu.VMEM((stages, RADIX - 1) + piece, link),
            pltpu.VMEM((n_space - 1,) + piece, link),
            pltpu.VMEM((max(stages - 1, 1),) + piece, link),
            pltpu.VMEM(piece, link),
            pltpu.VMEM(piece, jnp.float32),
            pltpu.SemaphoreType.DMA((stages, RADIX - 1)),
            pltpu.SemaphoreType.DMA((stages, RADIX - 1)),
            pltpu.SemaphoreType.DMA((n_space - 1,)),
            pltpu.SemaphoreType.DMA((n_space - 1,)),
        ],
        compiler_params=pltpu.CompilerParams(
            collective_id=collective_id,
            has_side_effects=True,
            vmem_limit_bytes=8 * 1024 * 1024,
        ),
    )(value.astype(link), base)


def gather_space(piece):
    count = lax.axis_size("space")
    place = lax.axis_index("space")
    rows = piece.shape[0]
    whole = jnp.zeros((count * rows,) + piece.shape[1:], piece.dtype)
    whole = lax.dynamic_update_slice_in_dim(whole, piece, place * rows, 0)
    for shift in range(1, count):
        part = lax.ppermute(
            piece, "space", [(i, (i + shift) % count) for i in range(count)]
        )
        source = (place + count - shift) % count
        whole = lax.dynamic_update_slice_in_dim(whole, part, source * rows, 0)
    return whole


def own_rows(whole, rows):
    return lax.dynamic_slice_in_dim(whole, lax.axis_index("space") * rows, rows, 0)


def on_device(input_field, weights, cotangent):
    rows = input_field.shape[0]
    channels = weights.shape[3]
    kernels = [w.reshape(3, 3, channels, channels) for w in weights]
    flipped = [k[::-1, ::-1] for k in kernels]
    full_input = gather_space(input_field)
    full_cotangent = gather_space(cotangent)

    begin_state = full_input
    for sweep_index in range(ITERS):
        block_end, _, _ = forward_block(begin_state, kernels)
        jump = own_rows(block_end - begin_state, rows)
        begin_state = scan_and_gather(jump, full_input, False, sweep_index)
    outputs, inputs_low, slopes = forward_block(begin_state, kernels)

    finish = full_cotangent
    for sweep_index in range(ITERS):
        begins, _ = backward_block(finish, flipped, slopes)
        back = own_rows(begins - finish, rows)
        finish = scan_and_gather(back, full_cotangent, True, ITERS + sweep_index)
    begins, scaled_list = backward_block(finish, flipped, slopes)

    quarter = channels // lax.axis_size("space")
    first = lax.axis_index("space") * quarter
    pieces = []
    for low, scaled in zip(inputs_low, scaled_list):
        signal = lax.dynamic_slice_in_dim(scaled, first, quarter, 2)
        grad = kernel_gradient(low, signal)
        pieces.append(jnp.transpose(grad, (3, 1, 2, 0)).reshape(quarter, 9, channels))
    weight_grad = jnp.stack(pieces, axis=1).astype(jnp.bfloat16)
    return (own_rows(outputs, rows)[None], own_rows(begins, rows)[None], weight_grad)


def solution(mesh):
    placed = (P("space", None, None), P("layer", None, None, None), P("space", None, None))
    return jax.shard_map(
        on_device,
        mesh=mesh,
        in_specs=placed,
        out_specs=(
            P("layer", "space", None, None),
            P("layer", "space", None, None),
            P("space", "layer", None, None),
        ),
        check_vma=False,
    )
```

```python
import functools

import jax
import jax.numpy as jnp
from jax import lax
from jax.experimental import pallas as pl
from jax.experimental.pallas import tpu as pltpu
from jax.sharding import PartitionSpec as P

MESH = pl.DeviceIdType.MESH

ITERS = 2
RADIX = 4
PIECES = 2

step_size = 0.125


CHUNK = 4


def column_chunks(low):
    height, width, channels = low.shape
    padded = jnp.pad(low, ((0, 0), (1, 1), (0, 0)))
    return jnp.stack(
        [padded[:, c : c + CHUNK + 2] for c in range(0, width, CHUNK)], axis=1
    )


def chunked_conv(low, kernel3, spec):
    height, width, channels = low.shape
    out = lax.conv_general_dilated(
        column_chunks(low),
        kernel3,
        (1, 1),
        ((1, 1), (0, 0)),
        dimension_numbers=("HNWC", spec, "HNWC"),
        preferred_element_type=jnp.float32,
    )
    return out.reshape(height, width, kernel3.shape[3] if spec == "HWIO" else kernel3.shape[2])


def conv(low, kernel3):
    return chunked_conv(low, kernel3, "HWIO")


def conv_transposed(low, flipped3):
    return chunked_conv(low, flipped3, "HWOI")


def kernel_gradient(low, signal):
    return lax.conv_general_dilated(
        low[None],
        signal[None],
        (1, 1),
        ((1, 1), (1, 1)),
        dimension_numbers=("CHWN", "IHWO", "NHWC"),
        preferred_element_type=jnp.float32,
    )


def forward_block(current, kernels):
    inputs_low = []
    slopes = []
    for kernel3 in kernels:
        low = current.astype(jnp.bfloat16)
        squashed = jnp.tanh(conv(low, kernel3))
        inputs_low.append(low)
        slopes.append(1.0 - squashed * squashed)
        current = current + step_size * squashed
    return current, inputs_low, slopes


def backward_block(adjoint, flipped, slopes):
    scaled_list = [None] * len(flipped)
    for index in reversed(range(len(flipped))):
        scaled = (step_size * slopes[index] * adjoint).astype(jnp.bfloat16)
        scaled_list[index] = scaled
        adjoint = adjoint + conv_transposed(scaled, flipped[index])
    return adjoint, scaled_list


def shifted_pairs(count, stride, shift):
    pairs = []
    for source in range(count):
        digit = (source // stride) % RADIX
        base = source - digit * stride
        pairs.append((source, base + ((digit + shift) % RADIX) * stride))
    return pairs


def exclusive_scan(value, reverse):
    count = lax.axis_size("layer")
    place = lax.axis_index("layer")
    total = jnp.zeros_like(value)
    stride = 1
    while stride < count:
        digit = (place // stride) % RADIX
        received = [
            lax.ppermute(value, "layer", shifted_pairs(count, stride, shift))
            for shift in range(1, RADIX)
        ]
        group = value
        for shift, part in zip(range(1, RADIX), received):
            earlier = shift > digit if reverse else shift <= digit
            total = total + jnp.where(earlier, part, jnp.zeros_like(part))
            group = group + part
        value = group
        stride *= RADIX
    return total


def scan_kernel(
    n_layer, n_space, n_piece, reverse, value_ref, base_ref, out_ref,
    slots, gathered, group_buf, mine, total, send_sems, recv_sems, gsend, grecv,
):
    layer = lax.axis_index("layer")
    space = lax.axis_index("space")
    rows = value_ref.shape[0]
    part_rows = rows // n_piece
    strides = []
    stride = 1
    while stride < n_layer:
        strides.append(stride)
        stride *= RADIX

    partners = []
    for stride in strides:
        digit = (layer // stride) % RADIX
        base = layer - digit * stride
        for shift in range(1, RADIX):
            partners.append((base + ((digit + shift) % RADIX) * stride, space))
    for shift in range(1, n_space):
        partners.append((layer, (space + shift) % n_space))
    barrier = pltpu.get_barrier_semaphore()
    for partner in partners:
        pl.semaphore_signal(barrier, inc=1, device_id=partner, device_id_type=MESH)
    pl.semaphore_wait(barrier, len(partners))

    for piece in range(n_piece):
        total[piece] = jnp.zeros(total.shape[1:], jnp.float32)
    pending = []
    sources = [value_ref.at[pl.ds(piece * part_rows, part_rows)] for piece in range(n_piece)]
    in_flight = {}

    def issue(piece, stage):
        if stage == len(strides):
            copies = []
            for shift in range(1, n_space):
                copy = pltpu.make_async_remote_copy(
                    src_ref=mine.at[piece],
                    dst_ref=gathered.at[piece, shift - 1],
                    send_sem=gsend.at[piece, shift - 1],
                    recv_sem=grecv.at[piece, shift - 1],
                    device_id=(layer, (space + shift) % n_space),
                    device_id_type=MESH,
                )
                copy.start()
                copies.append(copy)
                pending.append((copy, None))
            in_flight[piece] = copies
            return
        last = stage + 1 == len(strides)
        stride = strides[stage]
        digit = (layer // stride) % RADIX
        base = layer - digit * stride
        copies = []
        for shift in range(1, RADIX):
            copy = pltpu.make_async_remote_copy(
                src_ref=sources[piece],
                dst_ref=slots.at[piece, stage, shift - 1],
                send_sem=send_sems.at[piece, stage, shift - 1],
                recv_sem=recv_sems.at[piece, stage, shift - 1],
                device_id=(base + ((digit + shift) % RADIX) * stride, space),
                device_id_type=MESH,
            )
            wraps = digit + shift >= RADIX
            sends = (wraps if reverse else jnp.logical_not(wraps)) if last else None
            gets = (shift > digit if reverse else shift <= digit) if last else None
            if last:
                pl.when(sends)(copy.start)
            else:
                copy.start()
            copies.append((copy, gets))
            pending.append((copy, sends))
        in_flight[piece] = copies

    def finish(piece, stage):
        first = piece * part_rows
        if stage == len(strides):
            for copy in in_flight[piece]:
                copy.wait_recv()
            for shift in range(1, n_space):
                origin = (space + n_space - shift) % n_space
                there = pl.ds(origin * rows + first, part_rows)
                out_ref[there] = base_ref[there] + gathered[piece, shift - 1].astype(
                    jnp.float32
                )
            return
        last = stage + 1 == len(strides)
        stride = strides[stage]
        digit = (layer // stride) % RADIX
        for copy, gets in in_flight[piece]:
            if last:
                pl.when(gets)(copy.wait_recv)
            else:
                copy.wait_recv()
        group = sources[piece][...].astype(jnp.float32)
        for shift in range(1, RADIX):
            earlier = shift > digit if reverse else shift <= digit

            @pl.when(earlier)
            def _():
                total[piece] += slots[piece, stage, shift - 1].astype(jnp.float32)

            if not last:
                group = group + slots[piece, stage, shift - 1].astype(jnp.float32)
        if not last:
            group_buf[piece, stage] = group.astype(group_buf.dtype)
            sources[piece] = group_buf.at[piece, stage]
        else:
            mine[piece] = total[piece].astype(mine.dtype)
            here = pl.ds(space * rows + first, part_rows)
            out_ref[here] = base_ref[here] + total[piece]

    phases = len(strides) + 1
    for step in range(phases + n_piece - 1):
        active = [
            (piece, step - piece)
            for piece in range(n_piece)
            if 0 <= step - piece < phases
        ]
        for piece, stage in active:
            issue(piece, stage)
        for piece, stage in active:
            finish(piece, stage)
    for copy, sends in pending:
        if sends is None:
            copy.wait_send()
        else:
            pl.when(sends)(copy.wait_send)


def scan_and_gather(value, base, reverse, collective_id):
    n_layer = lax.axis_size("layer")
    n_space = lax.axis_size("space")
    stages = 0
    while RADIX ** stages < n_layer:
        stages += 1
    assert RADIX ** stages == n_layer
    rows, width, channels = value.shape
    n_piece = PIECES if rows % PIECES == 0 else 1
    piece = (rows // n_piece, width, channels)
    link = jnp.bfloat16
    return pl.pallas_call(
        functools.partial(scan_kernel, n_layer, n_space, n_piece, reverse),
        out_shape=jax.ShapeDtypeStruct((n_space * rows, width, channels), jnp.float32),
        in_specs=[pl.BlockSpec(memory_space=pltpu.VMEM)] * 2,
        out_specs=pl.BlockSpec(memory_space=pltpu.VMEM),
        scratch_shapes=[
            pltpu.VMEM((n_piece, stages, RADIX - 1) + piece, link),
            pltpu.VMEM((n_piece, n_space - 1) + piece, link),
            pltpu.VMEM((n_piece, max(stages - 1, 1)) + piece, link),
            pltpu.VMEM((n_piece,) + piece, link),
            pltpu.VMEM((n_piece,) + piece, jnp.float32),
            pltpu.SemaphoreType.DMA((n_piece, stages, RADIX - 1)),
            pltpu.SemaphoreType.DMA((n_piece, stages, RADIX - 1)),
            pltpu.SemaphoreType.DMA((n_piece, n_space - 1)),
            pltpu.SemaphoreType.DMA((n_piece, n_space - 1)),
        ],
        compiler_params=pltpu.CompilerParams(
            collective_id=collective_id,
            has_side_effects=True,
            vmem_limit_bytes=8 * 1024 * 1024,
        ),
    )(value.astype(link), base)


def gather_space(piece):
    count = lax.axis_size("space")
    place = lax.axis_index("space")
    rows = piece.shape[0]
    whole = jnp.zeros((count * rows,) + piece.shape[1:], piece.dtype)
    whole = lax.dynamic_update_slice_in_dim(whole, piece, place * rows, 0)
    for shift in range(1, count):
        part = lax.ppermute(
            piece, "space", [(i, (i + shift) % count) for i in range(count)]
        )
        source = (place + count - shift) % count
        whole = lax.dynamic_update_slice_in_dim(whole, part, source * rows, 0)
    return whole


def own_rows(whole, rows):
    return lax.dynamic_slice_in_dim(whole, lax.axis_index("space") * rows, rows, 0)


def on_device(input_field, weights, cotangent):
    rows = input_field.shape[0]
    channels = weights.shape[3]
    kernels = [w.reshape(3, 3, channels, channels) for w in weights]
    flipped = [k[::-1, ::-1] for k in kernels]
    full_input = gather_space(input_field)
    full_cotangent = gather_space(cotangent)

    begin_state = full_input
    for sweep_index in range(ITERS):
        block_end, _, _ = forward_block(begin_state, kernels)
        jump = own_rows(block_end - begin_state, rows)
        begin_state = scan_and_gather(jump, full_input, False, sweep_index)
    outputs, inputs_low, slopes = forward_block(begin_state, kernels)

    finish = full_cotangent
    for sweep_index in range(ITERS):
        begins, _ = backward_block(finish, flipped, slopes)
        back = own_rows(begins - finish, rows)
        finish = scan_and_gather(back, full_cotangent, True, ITERS + sweep_index)
    begins, scaled_list = backward_block(finish, flipped, slopes)

    quarter = channels // lax.axis_size("space")
    first = lax.axis_index("space") * quarter
    pieces = []
    for low, scaled in zip(inputs_low, scaled_list):
        signal = lax.dynamic_slice_in_dim(scaled, first, quarter, 2)
        grad = kernel_gradient(low, signal)
        pieces.append(jnp.transpose(grad, (3, 1, 2, 0)).reshape(quarter, 9, channels))
    weight_grad = jnp.stack(pieces, axis=1).astype(jnp.bfloat16)
    return (own_rows(outputs, rows)[None], own_rows(begins, rows)[None], weight_grad)


def solution(mesh):
    placed = (P("space", None, None), P("layer", None, None, None), P("space", None, None))
    return jax.shard_map(
        on_device,
        mesh=mesh,
        in_specs=placed,
        out_specs=(
            P("layer", "space", None, None),
            P("layer", "space", None, None),
            P("space", "layer", None, None),
        ),
        check_vma=False,
    )
```

```python
import functools

import jax
import jax.numpy as jnp
from jax import lax
from jax.experimental import pallas as pl
from jax.experimental.pallas import tpu as pltpu
from jax.sharding import PartitionSpec as P

MESH = pl.DeviceIdType.MESH

ITERS = 2
RADIX = 4

step_size = 0.125


CHUNK = 4


def column_chunks(low):
    height, width, channels = low.shape
    padded = jnp.pad(low, ((0, 0), (1, 1), (0, 0)))
    return jnp.stack(
        [padded[:, c : c + CHUNK + 2] for c in range(0, width, CHUNK)], axis=1
    )


def chunked_conv(low, kernel3, spec):
    height, width, channels = low.shape
    out = lax.conv_general_dilated(
        column_chunks(low),
        kernel3,
        (1, 1),
        ((1, 1), (0, 0)),
        dimension_numbers=("HNWC", spec, "HNWC"),
        preferred_element_type=jnp.float32,
    )
    return out.reshape(height, width, kernel3.shape[3] if spec == "HWIO" else kernel3.shape[2])


def conv(low, kernel3):
    return chunked_conv(low, kernel3, "HWIO")


def conv_transposed(low, flipped3):
    return chunked_conv(low, flipped3, "HWOI")


def kernel_gradient(low, signal):
    return lax.conv_general_dilated(
        low[None],
        signal[None],
        (1, 1),
        ((1, 1), (1, 1)),
        dimension_numbers=("CHWN", "IHWO", "CHWN"),
        preferred_element_type=jnp.float32,
    )


def forward_block(current, kernels):
    inputs_low = []
    slopes = []
    for kernel3 in kernels:
        low = current.astype(jnp.bfloat16)
        squashed = jnp.tanh(conv(low, kernel3))
        inputs_low.append(low)
        slopes.append(1.0 - squashed * squashed)
        current = current + step_size * squashed
    return current, inputs_low, slopes


def backward_block(adjoint, flipped, slopes):
    scaled_list = [None] * len(flipped)
    for index in reversed(range(len(flipped))):
        scaled = (step_size * slopes[index] * adjoint).astype(jnp.bfloat16)
        scaled_list[index] = scaled
        adjoint = adjoint + conv_transposed(scaled, flipped[index])
    return adjoint, scaled_list


def shifted_pairs(count, stride, shift):
    pairs = []
    for source in range(count):
        digit = (source // stride) % RADIX
        base = source - digit * stride
        pairs.append((source, base + ((digit + shift) % RADIX) * stride))
    return pairs


def exclusive_scan(value, reverse):
    count = lax.axis_size("layer")
    place = lax.axis_index("layer")
    total = jnp.zeros_like(value)
    stride = 1
    while stride < count:
        digit = (place // stride) % RADIX
        received = [
            lax.ppermute(value, "layer", shifted_pairs(count, stride, shift))
            for shift in range(1, RADIX)
        ]
        group = value
        for shift, part in zip(range(1, RADIX), received):
            earlier = shift > digit if reverse else shift <= digit
            total = total + jnp.where(earlier, part, jnp.zeros_like(part))
            group = group + part
        value = group
        stride *= RADIX
    return total


def scan_kernel(
    n_layer, n_space, reverse, value_ref, base_ref, out_ref,
    slots, gathered, group_buf, mine, total, send_sems, recv_sems, gsend, grecv,
):
    layer = lax.axis_index("layer")
    space = lax.axis_index("space")
    rows = value_ref.shape[0]
    strides = []
    stride = 1
    while stride < n_layer:
        strides.append(stride)
        stride *= RADIX

    partners = []
    for stride in strides:
        digit = (layer // stride) % RADIX
        base = layer - digit * stride
        for shift in range(1, RADIX):
            partners.append((base + ((digit + shift) % RADIX) * stride, space))
    for shift in range(1, n_space):
        partners.append((layer, (space + shift) % n_space))
    barrier = pltpu.get_barrier_semaphore()
    for partner in partners:
        pl.semaphore_signal(barrier, inc=1, device_id=partner, device_id_type=MESH)
    pl.semaphore_wait(barrier, len(partners))

    total[...] = jnp.zeros(total.shape, jnp.float32)
    pending = []
    source = value_ref
    for stage, stride in enumerate(strides):
        last = stage + 1 == len(strides)
        digit = (layer // stride) % RADIX
        base = layer - digit * stride
        copies = []
        for shift in range(1, RADIX):
            copy = pltpu.make_async_remote_copy(
                src_ref=source,
                dst_ref=slots.at[stage, shift - 1],
                send_sem=send_sems.at[stage, shift - 1],
                recv_sem=recv_sems.at[stage, shift - 1],
                device_id=(base + ((digit + shift) % RADIX) * stride, space),
                device_id_type=MESH,
            )
            wraps = digit + shift >= RADIX
            sends = (wraps if reverse else jnp.logical_not(wraps)) if last else None
            gets = (shift > digit if reverse else shift <= digit) if last else None
            copies.append((copy, sends, gets))
            if last:
                pl.when(sends)(copy.start)
            else:
                copy.start()
        for shift, (copy, sends, gets) in zip(range(1, RADIX), copies):
            if last:
                pl.when(gets)(copy.wait_recv)
            else:
                copy.wait_recv()
            pending.append((copy, sends))
        group = source[...].astype(jnp.float32)
        for shift in range(1, RADIX):
            earlier = shift > digit if reverse else shift <= digit

            @pl.when(earlier)
            def _():
                total[...] += slots[stage, shift - 1].astype(jnp.float32)

            if not last:
                group = group + slots[stage, shift - 1].astype(jnp.float32)
        if not last:
            group_buf[stage] = group.astype(group_buf.dtype)
            source = group_buf.at[stage]

    mine[...] = total[...].astype(mine.dtype)
    copies = []
    for shift in range(1, n_space):
        copy = pltpu.make_async_remote_copy(
            src_ref=mine,
            dst_ref=gathered.at[shift - 1],
            send_sem=gsend.at[shift - 1],
            recv_sem=grecv.at[shift - 1],
            device_id=(layer, (space + shift) % n_space),
            device_id_type=MESH,
        )
        copy.start()
        copies.append(copy)
    here = pl.ds(space * rows, rows)
    out_ref[here] = base_ref[here] + total[...]
    for copy in copies:
        copy.wait_recv()
    for shift in range(1, n_space):
        there = pl.ds(((space + n_space - shift) % n_space) * rows, rows)
        out_ref[there] = base_ref[there] + gathered[shift - 1].astype(jnp.float32)
    for copy, sends in pending:
        if sends is None:
            copy.wait_send()
        else:
            pl.when(sends)(copy.wait_send)
    for copy in copies:
        copy.wait_send()


def scan_and_gather(value, base, reverse, collective_id):
    n_layer = lax.axis_size("layer")
    n_space = lax.axis_size("space")
    stages = 0
    while RADIX ** stages < n_layer:
        stages += 1
    assert RADIX ** stages == n_layer
    rows, width, channels = value.shape
    piece = (rows, width, channels)
    link = jnp.bfloat16
    return pl.pallas_call(
        functools.partial(scan_kernel, n_layer, n_space, reverse),
        out_shape=jax.ShapeDtypeStruct((n_space * rows, width, channels), jnp.float32),
        in_specs=[pl.BlockSpec(memory_space=pltpu.VMEM)] * 2,
        out_specs=pl.BlockSpec(memory_space=pltpu.VMEM),
        scratch_shapes=[
            pltpu.VMEM((stages, RADIX - 1) + piece, link),
            pltpu.VMEM((n_space - 1,) + piece, link),
            pltpu.VMEM((max(stages - 1, 1),) + piece, link),
            pltpu.VMEM(piece, link),
            pltpu.VMEM(piece, jnp.float32),
            pltpu.SemaphoreType.DMA((stages, RADIX - 1)),
            pltpu.SemaphoreType.DMA((stages, RADIX - 1)),
            pltpu.SemaphoreType.DMA((n_space - 1,)),
            pltpu.SemaphoreType.DMA((n_space - 1,)),
        ],
        compiler_params=pltpu.CompilerParams(
            collective_id=collective_id,
            has_side_effects=True,
            vmem_limit_bytes=8 * 1024 * 1024,
        ),
    )(value.astype(link), base)


def gather_space(piece):
    count = lax.axis_size("space")
    place = lax.axis_index("space")
    rows = piece.shape[0]
    whole = jnp.zeros((count * rows,) + piece.shape[1:], piece.dtype)
    whole = lax.dynamic_update_slice_in_dim(whole, piece, place * rows, 0)
    low = piece.astype(jnp.bfloat16)
    for shift in range(1, count):
        part = lax.ppermute(
            low, "space", [(i, (i + shift) % count) for i in range(count)]
        ).astype(piece.dtype)
        source = (place + count - shift) % count
        whole = lax.dynamic_update_slice_in_dim(whole, part, source * rows, 0)
    return whole


def own_rows(whole, rows):
    return lax.dynamic_slice_in_dim(whole, lax.axis_index("space") * rows, rows, 0)


def on_device(input_field, weights, cotangent):
    rows = input_field.shape[0]
    channels = weights.shape[3]
    kernels = [w.reshape(3, 3, channels, channels) for w in weights]
    flipped = [k[::-1, ::-1] for k in kernels]
    full_input = gather_space(input_field)
    full_cotangent = gather_space(cotangent)

    begin_state = full_input
    for sweep_index in range(ITERS):
        block_end, _, _ = forward_block(begin_state, kernels)
        jump = own_rows(block_end - begin_state, rows)
        begin_state = scan_and_gather(jump, full_input, False, sweep_index)
    outputs, inputs_low, slopes = forward_block(begin_state, kernels)

    finish = full_cotangent
    for sweep_index in range(ITERS):
        begins, _ = backward_block(finish, flipped, slopes)
        back = own_rows(begins - finish, rows)
        finish = scan_and_gather(back, full_cotangent, True, ITERS + sweep_index)
    begins, scaled_list = backward_block(finish, flipped, slopes)

    quarter = channels // lax.axis_size("space")
    first = lax.axis_index("space") * quarter
    pieces = []
    for low, scaled in zip(inputs_low, scaled_list):
        signal = lax.dynamic_slice_in_dim(scaled, first, quarter, 2)
        grad = kernel_gradient(low, signal)
        pieces.append(grad.reshape(quarter, 9, channels))
    weight_grad = jnp.stack(pieces, axis=1).astype(jnp.bfloat16)
    return (own_rows(outputs, rows)[None], own_rows(begins, rows)[None], weight_grad)


def solution(mesh):
    placed = (P("space", None, None), P("layer", None, None, None), P("space", None, None))
    return jax.shard_map(
        on_device,
        mesh=mesh,
        in_specs=placed,
        out_specs=(
            P("layer", "space", None, None),
            P("layer", "space", None, None),
            P("space", "layer", None, None),
        ),
        check_vma=False,
    )
```

```python
import functools

import jax
import jax.numpy as jnp
from jax import lax
from jax.experimental import pallas as pl
from jax.experimental.pallas import tpu as pltpu
from jax.sharding import PartitionSpec as P

MESH = pl.DeviceIdType.MESH

ITERS = 2
RADIX = 4

step_size = 0.125


CHUNK = 4


def column_chunks(low):
    height, width, channels = low.shape
    padded = jnp.pad(low, ((0, 0), (1, 1), (0, 0)))
    return jnp.stack(
        [padded[:, c : c + CHUNK + 2] for c in range(0, width, CHUNK)], axis=1
    )


def chunked_conv(low, kernel3, spec):
    height, width, channels = low.shape
    out = lax.conv_general_dilated(
        column_chunks(low),
        kernel3,
        (1, 1),
        ((1, 1), (0, 0)),
        dimension_numbers=("HNWC", spec, "HNWC"),
        preferred_element_type=jnp.float32,
    )
    return out.reshape(height, width, kernel3.shape[3] if spec == "HWIO" else kernel3.shape[2])


def conv(low, kernel3):
    return chunked_conv(low, kernel3, "HWIO")


def conv_transposed(low, flipped3):
    return chunked_conv(low, flipped3, "HWOI")


def kernel_gradient(low, signal):
    return lax.conv_general_dilated(
        low[None],
        signal[None],
        (1, 1),
        ((1, 1), (1, 1)),
        dimension_numbers=("CHWN", "IHWO", "NHWC"),
        preferred_element_type=jnp.float32,
    )


def forward_block(current, kernels):
    inputs_low = []
    slopes = []
    for kernel3 in kernels:
        low = current.astype(jnp.bfloat16)
        squashed = jnp.tanh(conv(low, kernel3))
        inputs_low.append(low)
        slopes.append(1.0 - squashed * squashed)
        current = current + step_size * squashed
    return current, inputs_low, slopes


def backward_block(adjoint, flipped, slopes):
    scaled_list = [None] * len(flipped)
    for index in reversed(range(len(flipped))):
        scaled = (step_size * slopes[index] * adjoint).astype(jnp.bfloat16)
        scaled_list[index] = scaled
        adjoint = adjoint + conv_transposed(scaled, flipped[index])
    return adjoint, scaled_list


def shifted_pairs(count, stride, shift):
    pairs = []
    for source in range(count):
        digit = (source // stride) % RADIX
        base = source - digit * stride
        pairs.append((source, base + ((digit + shift) % RADIX) * stride))
    return pairs


def exclusive_scan(value, reverse):
    count = lax.axis_size("layer")
    place = lax.axis_index("layer")
    total = jnp.zeros_like(value)
    stride = 1
    while stride < count:
        digit = (place // stride) % RADIX
        received = [
            lax.ppermute(value, "layer", shifted_pairs(count, stride, shift))
            for shift in range(1, RADIX)
        ]
        group = value
        for shift, part in zip(range(1, RADIX), received):
            earlier = shift > digit if reverse else shift <= digit
            total = total + jnp.where(earlier, part, jnp.zeros_like(part))
            group = group + part
        value = group
        stride *= RADIX
    return total


def scan_kernel(
    n_layer, n_space, reverse, value_ref, base_ref, out_ref,
    slots, gathered, group_buf, mine, total, send_sems, recv_sems, gsend, grecv,
):
    layer = lax.axis_index("layer")
    space = lax.axis_index("space")
    rows = value_ref.shape[0]
    strides = []
    stride = 1
    while stride < n_layer:
        strides.append(stride)
        stride *= RADIX

    partners = []
    for stride in strides:
        digit = (layer // stride) % RADIX
        base = layer - digit * stride
        for shift in range(1, RADIX):
            partners.append((base + ((digit + shift) % RADIX) * stride, space))
    for shift in range(1, n_space):
        partners.append((layer, (space + shift) % n_space))
    barrier = pltpu.get_barrier_semaphore()
    for partner in partners:
        pl.semaphore_signal(barrier, inc=1, device_id=partner, device_id_type=MESH)
    pl.semaphore_wait(barrier, len(partners))

    total[...] = jnp.zeros(total.shape, jnp.float32)
    pending = []
    source = value_ref
    for stage, stride in enumerate(strides):
        last = stage + 1 == len(strides)
        digit = (layer // stride) % RADIX
        base = layer - digit * stride
        copies = []
        for shift in range(1, RADIX):
            copy = pltpu.make_async_remote_copy(
                src_ref=source,
                dst_ref=slots.at[stage, shift - 1],
                send_sem=send_sems.at[stage, shift - 1],
                recv_sem=recv_sems.at[stage, shift - 1],
                device_id=(base + ((digit + shift) % RADIX) * stride, space),
                device_id_type=MESH,
            )
            wraps = digit + shift >= RADIX
            sends = (wraps if reverse else jnp.logical_not(wraps)) if last else None
            gets = (shift > digit if reverse else shift <= digit) if last else None
            copies.append((copy, sends, gets))
            if last:
                pl.when(sends)(copy.start)
            else:
                copy.start()
        for shift, (copy, sends, gets) in zip(range(1, RADIX), copies):
            if last:
                pl.when(gets)(copy.wait_recv)
            else:
                copy.wait_recv()
            pending.append((copy, sends))
        group = source[...].astype(jnp.float32)
        for shift in range(1, RADIX):
            earlier = shift > digit if reverse else shift <= digit

            @pl.when(earlier)
            def _():
                total[...] += slots[stage, shift - 1].astype(jnp.float32)

            if not last:
                group = group + slots[stage, shift - 1].astype(jnp.float32)
        if not last:
            group_buf[stage] = group.astype(group_buf.dtype)
            source = group_buf.at[stage]

    mine[...] = total[...].astype(mine.dtype)
    copies = []
    for shift in range(1, n_space):
        copy = pltpu.make_async_remote_copy(
            src_ref=mine,
            dst_ref=gathered.at[shift - 1],
            send_sem=gsend.at[shift - 1],
            recv_sem=grecv.at[shift - 1],
            device_id=(layer, (space + shift) % n_space),
            device_id_type=MESH,
        )
        copy.start()
        copies.append(copy)
    here = pl.ds(space * rows, rows)
    out_ref[here] = base_ref[here] + total[...]
    for copy in copies:
        copy.wait_recv()
    for shift in range(1, n_space):
        there = pl.ds(((space + n_space - shift) % n_space) * rows, rows)
        out_ref[there] = base_ref[there] + gathered[shift - 1].astype(jnp.float32)
    for copy, sends in pending:
        if sends is None:
            copy.wait_send()
        else:
            pl.when(sends)(copy.wait_send)
    for copy in copies:
        copy.wait_send()


def scan_and_gather(value, base, reverse, collective_id):
    n_layer = lax.axis_size("layer")
    n_space = lax.axis_size("space")
    stages = 0
    while RADIX ** stages < n_layer:
        stages += 1
    assert RADIX ** stages == n_layer
    rows, width, channels = value.shape
    piece = (rows, width, channels)
    link = jnp.bfloat16
    return pl.pallas_call(
        functools.partial(scan_kernel, n_layer, n_space, reverse),
        out_shape=jax.ShapeDtypeStruct((n_space * rows, width, channels), jnp.float32),
        in_specs=[pl.BlockSpec(memory_space=pltpu.VMEM)] * 2,
        out_specs=pl.BlockSpec(memory_space=pltpu.VMEM),
        scratch_shapes=[
            pltpu.VMEM((stages, RADIX - 1) + piece, link),
            pltpu.VMEM((n_space - 1,) + piece, link),
            pltpu.VMEM((max(stages - 1, 1),) + piece, link),
            pltpu.VMEM(piece, link),
            pltpu.VMEM(piece, jnp.float32),
            pltpu.SemaphoreType.DMA((stages, RADIX - 1)),
            pltpu.SemaphoreType.DMA((stages, RADIX - 1)),
            pltpu.SemaphoreType.DMA((n_space - 1,)),
            pltpu.SemaphoreType.DMA((n_space - 1,)),
        ],
        compiler_params=pltpu.CompilerParams(
            collective_id=collective_id,
            has_side_effects=True,
            vmem_limit_bytes=8 * 1024 * 1024,
        ),
    )(value.astype(link), base)


def gather_space(piece):
    count = lax.axis_size("space")
    place = lax.axis_index("space")
    parts = [piece] + [
        lax.ppermute(piece, "space", [(i, (i + shift) % count) for i in range(count)])
        for shift in range(1, count)
    ]
    quarters = [
        lax.select_n((place + count - quarter) % count, *parts)
        for quarter in range(count)
    ]
    return jnp.concatenate(quarters, axis=0)


def own_rows(whole, rows):
    return lax.dynamic_slice_in_dim(whole, lax.axis_index("space") * rows, rows, 0)


def on_device(input_field, weights, cotangent):
    rows = input_field.shape[0]
    channels = weights.shape[3]
    kernels = [w.reshape(3, 3, channels, channels) for w in weights]
    flipped = [k[::-1, ::-1] for k in kernels]
    full_input = gather_space(input_field)
    full_cotangent = gather_space(cotangent)

    begin_state = full_input
    for sweep_index in range(ITERS):
        block_end, _, _ = forward_block(begin_state, kernels)
        jump = own_rows(block_end - begin_state, rows)
        begin_state = scan_and_gather(jump, full_input, False, sweep_index)
    outputs, inputs_low, slopes = forward_block(begin_state, kernels)

    finish = full_cotangent
    for sweep_index in range(ITERS):
        begins, _ = backward_block(finish, flipped, slopes)
        back = own_rows(begins - finish, rows)
        finish = scan_and_gather(back, full_cotangent, True, ITERS + sweep_index)
    begins, scaled_list = backward_block(finish, flipped, slopes)

    quarter = channels // lax.axis_size("space")
    first = lax.axis_index("space") * quarter
    pieces = []
    for low, scaled in zip(inputs_low, scaled_list):
        signal = lax.dynamic_slice_in_dim(scaled, first, quarter, 2)
        grad = kernel_gradient(low, signal)
        pieces.append(jnp.transpose(grad, (3, 1, 2, 0)).reshape(quarter, 9, channels))
    weight_grad = jnp.stack(pieces, axis=1).astype(jnp.bfloat16)
    return (own_rows(outputs, rows)[None], own_rows(begins, rows)[None], weight_grad)


def solution(mesh):
    placed = (P("space", None, None), P("layer", None, None, None), P("space", None, None))
    return jax.shard_map(
        on_device,
        mesh=mesh,
        in_specs=placed,
        out_specs=(
            P("layer", "space", None, None),
            P("layer", "space", None, None),
            P("space", "layer", None, None),
        ),
        check_vma=False,
    )
```

```python
import functools

import jax
import jax.numpy as jnp
from jax import lax
from jax.experimental import pallas as pl
from jax.experimental.pallas import tpu as pltpu
from jax.sharding import PartitionSpec as P

MESH = pl.DeviceIdType.MESH

ITERS = 2
RADIX = 4

step_size = 0.125


CHUNK = 4


def column_chunks(low):
    height, width, channels = low.shape
    padded = jnp.pad(low, ((0, 0), (1, 1), (0, 0)))
    return jnp.stack(
        [padded[:, c : c + CHUNK + 2] for c in range(0, width, CHUNK)], axis=1
    )


def chunked_conv(low, kernel3, spec):
    height, width, channels = low.shape
    out = lax.conv_general_dilated(
        column_chunks(low),
        kernel3,
        (1, 1),
        ((1, 1), (0, 0)),
        dimension_numbers=("HNWC", spec, "HNWC"),
        preferred_element_type=jnp.float32,
    )
    return out.reshape(height, width, kernel3.shape[3] if spec == "HWIO" else kernel3.shape[2])


def conv(low, kernel3):
    return chunked_conv(low, kernel3, "HWIO")


def conv_transposed(low, flipped3):
    return chunked_conv(low, flipped3, "HWOI")


def kernel_gradient(low, signal):
    return lax.conv_general_dilated(
        low[None],
        signal[None],
        (1, 1),
        ((1, 1), (1, 1)),
        dimension_numbers=("CHWN", "IHWO", "NHWC"),
        preferred_element_type=jnp.float32,
    )


def forward_block(current, kernels):
    inputs_low = []
    slopes = []
    for kernel3 in kernels:
        low = current.astype(jnp.bfloat16)
        squashed = jnp.tanh(conv(low, kernel3))
        inputs_low.append(low)
        slopes.append(1.0 - squashed * squashed)
        current = current + step_size * squashed
    return current, inputs_low, slopes


def backward_block(adjoint, flipped, slopes):
    scaled_list = [None] * len(flipped)
    for index in reversed(range(len(flipped))):
        scaled = (step_size * slopes[index] * adjoint).astype(jnp.bfloat16)
        scaled_list[index] = scaled
        adjoint = adjoint + conv_transposed(scaled, flipped[index])
    return adjoint, scaled_list


def shifted_pairs(count, stride, shift):
    pairs = []
    for source in range(count):
        digit = (source // stride) % RADIX
        base = source - digit * stride
        pairs.append((source, base + ((digit + shift) % RADIX) * stride))
    return pairs


def exclusive_scan(value, reverse):
    count = lax.axis_size("layer")
    place = lax.axis_index("layer")
    total = jnp.zeros_like(value)
    stride = 1
    while stride < count:
        digit = (place // stride) % RADIX
        received = [
            lax.ppermute(value, "layer", shifted_pairs(count, stride, shift))
            for shift in range(1, RADIX)
        ]
        group = value
        for shift, part in zip(range(1, RADIX), received):
            earlier = shift > digit if reverse else shift <= digit
            total = total + jnp.where(earlier, part, jnp.zeros_like(part))
            group = group + part
        value = group
        stride *= RADIX
    return total


def scan_kernel(
    n_layer, n_space, reverse, value_ref, base_ref, out_ref,
    slots, gathered, group_buf, mine, total, send_sems, recv_sems, gsend, grecv,
):
    layer = lax.axis_index("layer")
    space = lax.axis_index("space")
    rows = value_ref.shape[0]
    strides = []
    stride = 1
    while stride < n_layer:
        strides.append(stride)
        stride *= RADIX

    partners = []
    for stride in strides:
        digit = (layer // stride) % RADIX
        base = layer - digit * stride
        for shift in range(1, RADIX):
            partners.append((base + ((digit + shift) % RADIX) * stride, space))
    for shift in range(1, n_space):
        partners.append((layer, (space + shift) % n_space))
    barrier = pltpu.get_barrier_semaphore()
    for partner in partners:
        pl.semaphore_signal(barrier, inc=1, device_id=partner, device_id_type=MESH)
    pl.semaphore_wait(barrier, len(partners))

    total[...] = jnp.zeros(total.shape, jnp.float32)
    pending = []
    source = value_ref
    for stage, stride in enumerate(strides):
        last = stage + 1 == len(strides)
        digit = (layer // stride) % RADIX
        base = layer - digit * stride
        copies = []
        for shift in range(1, RADIX):
            copy = pltpu.make_async_remote_copy(
                src_ref=source,
                dst_ref=slots.at[stage, shift - 1],
                send_sem=send_sems.at[stage, shift - 1],
                recv_sem=recv_sems.at[stage, shift - 1],
                device_id=(base + ((digit + shift) % RADIX) * stride, space),
                device_id_type=MESH,
            )
            wraps = digit + shift >= RADIX
            sends = (wraps if reverse else jnp.logical_not(wraps)) if last else None
            gets = (shift > digit if reverse else shift <= digit) if last else None
            copies.append((copy, sends, gets))
            if last:
                pl.when(sends)(copy.start)
            else:
                copy.start()
        for shift, (copy, sends, gets) in zip(range(1, RADIX), copies):
            if last:
                pl.when(gets)(copy.wait_recv)
            else:
                copy.wait_recv()
            pending.append((copy, sends))
        group = source[...].astype(jnp.float32)
        for shift in range(1, RADIX):
            earlier = shift > digit if reverse else shift <= digit

            @pl.when(earlier)
            def _():
                total[...] += slots[stage, shift - 1].astype(jnp.float32)

            if not last:
                group = group + slots[stage, shift - 1].astype(jnp.float32)
        if not last:
            group_buf[stage] = group.astype(group_buf.dtype)
            source = group_buf.at[stage]

    mine[...] = total[...].astype(mine.dtype)
    copies = []
    for shift in range(1, n_space):
        copy = pltpu.make_async_remote_copy(
            src_ref=mine,
            dst_ref=gathered.at[shift - 1],
            send_sem=gsend.at[shift - 1],
            recv_sem=grecv.at[shift - 1],
            device_id=(layer, (space + shift) % n_space),
            device_id_type=MESH,
        )
        copy.start()
        copies.append(copy)
    here = pl.ds(space * rows, rows)
    out_ref[here] = base_ref[here] + total[...]
    for copy in copies:
        copy.wait_recv()
    for shift in range(1, n_space):
        there = pl.ds(((space + n_space - shift) % n_space) * rows, rows)
        out_ref[there] = base_ref[there] + gathered[shift - 1].astype(jnp.float32)
    for copy, sends in pending:
        if sends is None:
            copy.wait_send()
        else:
            pl.when(sends)(copy.wait_send)
    for copy in copies:
        copy.wait_send()


def scan_and_gather(value, base, reverse, collective_id):
    n_layer = lax.axis_size("layer")
    n_space = lax.axis_size("space")
    stages = 0
    while RADIX ** stages < n_layer:
        stages += 1
    assert RADIX ** stages == n_layer
    rows, width, channels = value.shape
    piece = (rows, width, channels)
    link = jnp.bfloat16
    return pl.pallas_call(
        functools.partial(scan_kernel, n_layer, n_space, reverse),
        out_shape=jax.ShapeDtypeStruct((n_space * rows, width, channels), jnp.float32),
        in_specs=[pl.BlockSpec(memory_space=pltpu.VMEM)] * 2,
        out_specs=pl.BlockSpec(memory_space=pltpu.VMEM),
        scratch_shapes=[
            pltpu.VMEM((stages, RADIX - 1) + piece, link),
            pltpu.VMEM((n_space - 1,) + piece, link),
            pltpu.VMEM((max(stages - 1, 1),) + piece, link),
            pltpu.VMEM(piece, link),
            pltpu.VMEM(piece, jnp.float32),
            pltpu.SemaphoreType.DMA((stages, RADIX - 1)),
            pltpu.SemaphoreType.DMA((stages, RADIX - 1)),
            pltpu.SemaphoreType.DMA((n_space - 1,)),
            pltpu.SemaphoreType.DMA((n_space - 1,)),
        ],
        compiler_params=pltpu.CompilerParams(
            collective_id=collective_id,
            has_side_effects=True,
            vmem_limit_bytes=8 * 1024 * 1024,
        ),
    )(value.astype(link), base)


def gather_space(piece):
    count = lax.axis_size("space")
    place = lax.axis_index("space")
    rows = piece.shape[0]
    whole = jnp.zeros((count * rows,) + piece.shape[1:], piece.dtype)
    whole = lax.dynamic_update_slice_in_dim(whole, piece, place * rows, 0)
    for shift in range(1, count):
        part = lax.ppermute(
            piece, "space", [(i, (i + shift) % count) for i in range(count)]
        )
        source = (place + count - shift) % count
        whole = lax.dynamic_update_slice_in_dim(whole, part, source * rows, 0)
    return whole


def own_jump(piece, kernels):
    count = lax.axis_size("space")
    place = lax.axis_index("space")
    rows = piece.shape[0]
    halo = len(kernels)
    assert halo <= rows
    top = lax.ppermute(piece[rows - halo :], "space", [(i, i + 1) for i in range(count - 1)])
    bottom = lax.ppermute(piece[:halo], "space", [(i + 1, i) for i in range(count - 1)])
    start = jnp.concatenate([top, piece, bottom], axis=0)
    index = place * rows - halo + jnp.arange(rows + 2 * halo)
    inside = ((index >= 0) & (index < rows * count))[:, None, None]
    current = start
    for kernel3 in kernels:
        low = jnp.where(inside, current, jnp.zeros_like(current)).astype(jnp.bfloat16)
        current = current + step_size * jnp.tanh(conv(low, kernel3))
    return (current - start)[halo : halo + rows]


def own_rows(whole, rows):
    return lax.dynamic_slice_in_dim(whole, lax.axis_index("space") * rows, rows, 0)


def on_device(input_field, weights, cotangent):
    rows = input_field.shape[0]
    channels = weights.shape[3]
    kernels = [w.reshape(3, 3, channels, channels) for w in weights]
    flipped = [k[::-1, ::-1] for k in kernels]
    full_input = gather_space(input_field)
    full_cotangent = gather_space(cotangent)

    begin_state = full_input
    for sweep_index in range(ITERS):
        if sweep_index == 0:
            jump = own_jump(input_field, kernels)
        else:
            block_end, _, _ = forward_block(begin_state, kernels)
            jump = own_rows(block_end - begin_state, rows)
        begin_state = scan_and_gather(jump, full_input, False, sweep_index)
    outputs, inputs_low, slopes = forward_block(begin_state, kernels)

    finish = full_cotangent
    for sweep_index in range(ITERS):
        begins, _ = backward_block(finish, flipped, slopes)
        back = own_rows(begins - finish, rows)
        finish = scan_and_gather(back, full_cotangent, True, ITERS + sweep_index)
    begins, scaled_list = backward_block(finish, flipped, slopes)

    quarter = channels // lax.axis_size("space")
    first = lax.axis_index("space") * quarter
    pieces = []
    for low, scaled in zip(inputs_low, scaled_list):
        signal = lax.dynamic_slice_in_dim(scaled, first, quarter, 2)
        grad = kernel_gradient(low, signal)
        pieces.append(jnp.transpose(grad, (3, 1, 2, 0)).reshape(quarter, 9, channels))
    weight_grad = jnp.stack(pieces, axis=1).astype(jnp.bfloat16)
    return (own_rows(outputs, rows)[None], own_rows(begins, rows)[None], weight_grad)


def solution(mesh):
    placed = (P("space", None, None), P("layer", None, None, None), P("space", None, None))
    return jax.shard_map(
        on_device,
        mesh=mesh,
        in_specs=placed,
        out_specs=(
            P("layer", "space", None, None),
            P("layer", "space", None, None),
            P("space", "layer", None, None),
        ),
        check_vma=False,
    )
```

```python
import functools

import jax
import jax.numpy as jnp
from jax import lax
from jax.experimental import pallas as pl
from jax.experimental.pallas import tpu as pltpu
from jax.sharding import PartitionSpec as P

MESH = pl.DeviceIdType.MESH

ITERS = 2
RADIX = 4

step_size = 0.125


CHUNK = 4


def column_chunks(low):
    height, width, channels = low.shape
    padded = jnp.pad(low, ((0, 0), (1, 1), (0, 0)))
    return jnp.stack(
        [padded[:, c : c + CHUNK + 2] for c in range(0, width, CHUNK)], axis=1
    )


def chunked_conv(low, kernel3, spec):
    height, width, channels = low.shape
    out = lax.conv_general_dilated(
        column_chunks(low),
        kernel3,
        (1, 1),
        ((1, 1), (0, 0)),
        dimension_numbers=("HNWC", spec, "HNWC"),
        preferred_element_type=jnp.float32,
    )
    return out.reshape(height, width, kernel3.shape[3] if spec == "HWIO" else kernel3.shape[2])


def conv(low, kernel3):
    return chunked_conv(low, kernel3, "HWIO")


def conv_transposed(low, flipped3):
    return chunked_conv(low, flipped3, "HWOI")


def kernel_gradient(low, signal):
    return lax.conv_general_dilated(
        low[None],
        signal[None],
        (1, 1),
        ((1, 1), (1, 1)),
        dimension_numbers=("CHWN", "IHWO", "NHWC"),
        preferred_element_type=jnp.float32,
    )


def forward_block(current, kernels):
    inputs_low = []
    slopes = []
    for kernel3 in kernels:
        low = current.astype(jnp.bfloat16)
        squashed = jnp.tanh(conv(low, kernel3))
        inputs_low.append(low)
        slopes.append(1.0 - squashed * squashed)
        current = current + step_size * squashed
    return current, inputs_low, slopes


def backward_block(adjoint, flipped, slopes):
    scaled_list = [None] * len(flipped)
    for index in reversed(range(len(flipped))):
        scaled = (step_size * slopes[index] * adjoint).astype(jnp.bfloat16)
        scaled_list[index] = scaled
        adjoint = adjoint + conv_transposed(scaled, flipped[index])
    return adjoint, scaled_list


def shifted_pairs(count, stride, shift):
    pairs = []
    for source in range(count):
        digit = (source // stride) % RADIX
        base = source - digit * stride
        pairs.append((source, base + ((digit + shift) % RADIX) * stride))
    return pairs


def exclusive_scan(value, reverse):
    count = lax.axis_size("layer")
    place = lax.axis_index("layer")
    total = jnp.zeros_like(value)
    stride = 1
    while stride < count:
        digit = (place // stride) % RADIX
        received = [
            lax.ppermute(value, "layer", shifted_pairs(count, stride, shift))
            for shift in range(1, RADIX)
        ]
        group = value
        for shift, part in zip(range(1, RADIX), received):
            earlier = shift > digit if reverse else shift <= digit
            total = total + jnp.where(earlier, part, jnp.zeros_like(part))
            group = group + part
        value = group
        stride *= RADIX
    return total


def scan_kernel(
    n_layer, n_space, reverse, value_ref, base_ref, out_ref,
    slots, gathered, group_buf, mine, total, send_sems, recv_sems, gsend, grecv,
):
    layer = lax.axis_index("layer")
    space = lax.axis_index("space")
    rows = value_ref.shape[0]
    strides = []
    stride = 1
    while stride < n_layer:
        strides.append(stride)
        stride *= RADIX

    partners = []
    for stride in strides:
        digit = (layer // stride) % RADIX
        base = layer - digit * stride
        for shift in range(1, RADIX):
            partners.append((base + ((digit + shift) % RADIX) * stride, space))
    for shift in range(1, n_space):
        partners.append((layer, (space + shift) % n_space))
    barrier = pltpu.get_barrier_semaphore()
    for partner in partners:
        pl.semaphore_signal(barrier, inc=1, device_id=partner, device_id_type=MESH)
    pl.semaphore_wait(barrier, len(partners))

    total[...] = jnp.zeros(total.shape, jnp.float32)
    pending = []
    source = value_ref
    for stage, stride in enumerate(strides):
        last = stage + 1 == len(strides)
        digit = (layer // stride) % RADIX
        base = layer - digit * stride
        copies = []
        for shift in range(1, RADIX):
            copy = pltpu.make_async_remote_copy(
                src_ref=source,
                dst_ref=slots.at[stage, shift - 1],
                send_sem=send_sems.at[stage, shift - 1],
                recv_sem=recv_sems.at[stage, shift - 1],
                device_id=(base + ((digit + shift) % RADIX) * stride, space),
                device_id_type=MESH,
            )
            wraps = digit + shift >= RADIX
            sends = (wraps if reverse else jnp.logical_not(wraps)) if last else None
            gets = (shift > digit if reverse else shift <= digit) if last else None
            copies.append((copy, sends, gets))
            if last:
                pl.when(sends)(copy.start)
            else:
                copy.start()
        for shift, (copy, sends, gets) in zip(range(1, RADIX), copies):
            if last:
                pl.when(gets)(copy.wait_recv)
            else:
                copy.wait_recv()
            pending.append((copy, sends))
        group = source[...].astype(jnp.float32)
        for shift in range(1, RADIX):
            earlier = shift > digit if reverse else shift <= digit

            @pl.when(earlier)
            def _():
                total[...] += slots[stage, shift - 1].astype(jnp.float32)

            if not last:
                group = group + slots[stage, shift - 1].astype(jnp.float32)
        if not last:
            group_buf[stage] = group.astype(group_buf.dtype)
            source = group_buf.at[stage]

    mine[...] = total[...].astype(mine.dtype)
    copies = []
    for shift in range(1, n_space):
        copy = pltpu.make_async_remote_copy(
            src_ref=mine,
            dst_ref=gathered.at[shift - 1],
            send_sem=gsend.at[shift - 1],
            recv_sem=grecv.at[shift - 1],
            device_id=(layer, (space + shift) % n_space),
            device_id_type=MESH,
        )
        copy.start()
        copies.append(copy)
    here = pl.ds(space * rows, rows)
    out_ref[here] = base_ref[here] + total[...]
    for copy in copies:
        copy.wait_recv()
    for shift in range(1, n_space):
        there = pl.ds(((space + n_space - shift) % n_space) * rows, rows)
        out_ref[there] = base_ref[there] + gathered[shift - 1].astype(jnp.float32)
    for copy, sends in pending:
        if sends is None:
            copy.wait_send()
        else:
            pl.when(sends)(copy.wait_send)
    for copy in copies:
        copy.wait_send()


def scan_and_gather(value, base, reverse, collective_id):
    n_layer = lax.axis_size("layer")
    n_space = lax.axis_size("space")
    stages = 0
    while RADIX ** stages < n_layer:
        stages += 1
    assert RADIX ** stages == n_layer
    rows, width, channels = value.shape
    piece = (rows, width, channels)
    link = jnp.bfloat16
    return pl.pallas_call(
        functools.partial(scan_kernel, n_layer, n_space, reverse),
        out_shape=jax.ShapeDtypeStruct((n_space * rows, width, channels), jnp.float32),
        in_specs=[pl.BlockSpec(memory_space=pltpu.VMEM)] * 2,
        out_specs=pl.BlockSpec(memory_space=pltpu.VMEM),
        scratch_shapes=[
            pltpu.VMEM((stages, RADIX - 1) + piece, link),
            pltpu.VMEM((n_space - 1,) + piece, link),
            pltpu.VMEM((max(stages - 1, 1),) + piece, link),
            pltpu.VMEM(piece, link),
            pltpu.VMEM(piece, jnp.float32),
            pltpu.SemaphoreType.DMA((stages, RADIX - 1)),
            pltpu.SemaphoreType.DMA((stages, RADIX - 1)),
            pltpu.SemaphoreType.DMA((n_space - 1,)),
            pltpu.SemaphoreType.DMA((n_space - 1,)),
        ],
        compiler_params=pltpu.CompilerParams(
            collective_id=collective_id,
            has_side_effects=True,
            vmem_limit_bytes=8 * 1024 * 1024,
        ),
    )(value.astype(link), base)


def gather_space(piece):
    count = lax.axis_size("space")
    place = lax.axis_index("space")
    rows = piece.shape[0]
    whole = jnp.zeros((count * rows,) + piece.shape[1:], piece.dtype)
    whole = lax.dynamic_update_slice_in_dim(whole, piece, place * rows, 0)
    for shift in range(1, count):
        part = lax.ppermute(
            piece, "space", [(i, (i + shift) % count) for i in range(count)]
        )
        source = (place + count - shift) % count
        whole = lax.dynamic_update_slice_in_dim(whole, part, source * rows, 0)
    return whole


def own_rows(whole, rows):
    return lax.dynamic_slice_in_dim(whole, lax.axis_index("space") * rows, rows, 0)


def on_device(input_field, weights, cotangent):
    rows = input_field.shape[0]
    channels = weights.shape[3]
    kernels = [w.reshape(3, 3, channels, channels) for w in weights]
    flipped = [k[::-1, ::-1] for k in kernels]
    both = gather_space(jnp.stack([input_field, cotangent], axis=1))
    full_input = both[:, 0]
    full_cotangent = both[:, 1]

    begin_state = full_input
    for sweep_index in range(ITERS):
        block_end, _, _ = forward_block(begin_state, kernels)
        jump = own_rows(block_end - begin_state, rows)
        begin_state = scan_and_gather(jump, full_input, False, sweep_index)
    outputs, inputs_low, slopes = forward_block(begin_state, kernels)

    finish = full_cotangent
    for sweep_index in range(ITERS):
        begins, _ = backward_block(finish, flipped, slopes)
        back = own_rows(begins - finish, rows)
        finish = scan_and_gather(back, full_cotangent, True, ITERS + sweep_index)
    begins, scaled_list = backward_block(finish, flipped, slopes)

    quarter = channels // lax.axis_size("space")
    first = lax.axis_index("space") * quarter
    pieces = []
    for low, scaled in zip(inputs_low, scaled_list):
        signal = lax.dynamic_slice_in_dim(scaled, first, quarter, 2)
        grad = kernel_gradient(low, signal)
        pieces.append(jnp.transpose(grad, (3, 1, 2, 0)).reshape(quarter, 9, channels))
    weight_grad = jnp.stack(pieces, axis=1).astype(jnp.bfloat16)
    return (own_rows(outputs, rows)[None], own_rows(begins, rows)[None], weight_grad)


def solution(mesh):
    placed = (P("space", None, None), P("layer", None, None, None), P("space", None, None))
    return jax.shard_map(
        on_device,
        mesh=mesh,
        in_specs=placed,
        out_specs=(
            P("layer", "space", None, None),
            P("layer", "space", None, None),
            P("space", "layer", None, None),
        ),
        check_vma=False,
    )
```

```python
import functools

import jax
import jax.numpy as jnp
from jax import lax
from jax.experimental import pallas as pl
from jax.experimental.pallas import tpu as pltpu
from jax.sharding import PartitionSpec as P

MESH = pl.DeviceIdType.MESH

ITERS = 2
RADIX = 4

step_size = 0.125


CHUNK = 4


def column_chunks(low):
    height, width, channels = low.shape
    padded = jnp.pad(low, ((0, 0), (1, 1), (0, 0)))
    return jnp.stack(
        [padded[:, c : c + CHUNK + 2] for c in range(0, width, CHUNK)], axis=1
    )


def chunked_conv(low, kernel3, spec):
    height, width, channels = low.shape
    out = lax.conv_general_dilated(
        column_chunks(low),
        kernel3,
        (1, 1),
        ((1, 1), (0, 0)),
        dimension_numbers=("HNWC", spec, "HNWC"),
        preferred_element_type=jnp.float32,
    )
    return out.reshape(height, width, kernel3.shape[3] if spec == "HWIO" else kernel3.shape[2])


def conv(low, kernel3):
    return chunked_conv(low, kernel3, "HWIO")


def conv_transposed(low, flipped3):
    return chunked_conv(low, flipped3, "HWOI")


def kernel_gradient(low, signal):
    return lax.conv_general_dilated(
        low[None],
        signal[None],
        (1, 1),
        ((1, 1), (1, 1)),
        dimension_numbers=("CHWN", "IHWO", "NHWC"),
        preferred_element_type=jnp.float32,
    )


def forward_block(current, kernels):
    inputs_low = []
    slopes = []
    for kernel3 in kernels:
        low = current.astype(jnp.bfloat16)
        squashed = jnp.tanh(conv(low, kernel3))
        inputs_low.append(low)
        slopes.append(1.0 - squashed * squashed)
        current = current + step_size * squashed
    return current, inputs_low, slopes


def backward_block(adjoint, flipped, slopes):
    scaled_list = [None] * len(flipped)
    for index in reversed(range(len(flipped))):
        scaled = (step_size * slopes[index] * adjoint).astype(jnp.bfloat16)
        scaled_list[index] = scaled
        adjoint = adjoint + conv_transposed(scaled, flipped[index])
    return adjoint, scaled_list


def shifted_pairs(count, stride, shift):
    pairs = []
    for source in range(count):
        digit = (source // stride) % RADIX
        base = source - digit * stride
        pairs.append((source, base + ((digit + shift) % RADIX) * stride))
    return pairs


def exclusive_scan(value, reverse):
    count = lax.axis_size("layer")
    place = lax.axis_index("layer")
    total = jnp.zeros_like(value)
    stride = 1
    while stride < count:
        digit = (place // stride) % RADIX
        received = [
            lax.ppermute(value, "layer", shifted_pairs(count, stride, shift))
            for shift in range(1, RADIX)
        ]
        group = value
        for shift, part in zip(range(1, RADIX), received):
            earlier = shift > digit if reverse else shift <= digit
            total = total + jnp.where(earlier, part, jnp.zeros_like(part))
            group = group + part
        value = group
        stride *= RADIX
    return total


def scan_kernel(
    n_layer, n_space, reverse, value_ref, base_ref, out_ref,
    slots, gathered, group_buf, mine, total, send_sems, recv_sems, gsend, grecv,
):
    layer = lax.axis_index("layer")
    space = lax.axis_index("space")
    rows = value_ref.shape[0]
    strides = []
    stride = 1
    while stride < n_layer:
        strides.append(stride)
        stride *= RADIX

    partners = []
    for stride in strides:
        digit = (layer // stride) % RADIX
        base = layer - digit * stride
        for shift in range(1, RADIX):
            partners.append((base + ((digit + shift) % RADIX) * stride, space))
    for shift in range(1, n_space):
        partners.append((layer, (space + shift) % n_space))
    barrier = pltpu.get_barrier_semaphore()
    for partner in partners:
        pl.semaphore_signal(barrier, inc=1, device_id=partner, device_id_type=MESH)
    pl.semaphore_wait(barrier, len(partners))

    total[...] = jnp.zeros(total.shape, jnp.float32)
    pending = []
    source = value_ref
    for stage, stride in enumerate(strides):
        last = stage + 1 == len(strides)
        digit = (layer // stride) % RADIX
        base = layer - digit * stride
        copies = []
        for shift in range(1, RADIX):
            copy = pltpu.make_async_remote_copy(
                src_ref=source,
                dst_ref=slots.at[stage, shift - 1],
                send_sem=send_sems.at[stage, shift - 1],
                recv_sem=recv_sems.at[stage, shift - 1],
                device_id=(base + ((digit + shift) % RADIX) * stride, space),
                device_id_type=MESH,
            )
            wraps = digit + shift >= RADIX
            sends = (wraps if reverse else jnp.logical_not(wraps)) if last else None
            gets = (shift > digit if reverse else shift <= digit) if last else None
            copies.append((copy, sends, gets))
            if last:
                pl.when(sends)(copy.start)
            else:
                copy.start()
        for shift, (copy, sends, gets) in zip(range(1, RADIX), copies):
            if last:
                pl.when(gets)(copy.wait_recv)
            else:
                copy.wait_recv()
            pending.append((copy, sends))
        group = source[...].astype(jnp.float32)
        for shift in range(1, RADIX):
            earlier = shift > digit if reverse else shift <= digit

            @pl.when(earlier)
            def _():
                total[...] += slots[stage, shift - 1].astype(jnp.float32)

            if not last:
                group = group + slots[stage, shift - 1].astype(jnp.float32)
        if not last:
            group_buf[stage] = group.astype(group_buf.dtype)
            source = group_buf.at[stage]

    mine[...] = total[...].astype(mine.dtype)
    copies = []
    for shift in range(1, n_space):
        copy = pltpu.make_async_remote_copy(
            src_ref=mine,
            dst_ref=gathered.at[shift - 1],
            send_sem=gsend.at[shift - 1],
            recv_sem=grecv.at[shift - 1],
            device_id=(layer, (space + shift) % n_space),
            device_id_type=MESH,
        )
        copy.start()
        copies.append(copy)
    here = pl.ds(space * rows, rows)
    out_ref[here] = base_ref[here] + total[...]
    for copy in copies:
        copy.wait_recv()
    for shift in range(1, n_space):
        there = pl.ds(((space + n_space - shift) % n_space) * rows, rows)
        out_ref[there] = base_ref[there] + gathered[shift - 1].astype(jnp.float32)
    for copy, sends in pending:
        if sends is None:
            copy.wait_send()
        else:
            pl.when(sends)(copy.wait_send)
    for copy in copies:
        copy.wait_send()


def scan_and_gather(value, base, reverse, collective_id):
    n_layer = lax.axis_size("layer")
    n_space = lax.axis_size("space")
    stages = 0
    while RADIX ** stages < n_layer:
        stages += 1
    assert RADIX ** stages == n_layer
    rows, width, channels = value.shape
    piece = (rows, width, channels)
    link = jnp.bfloat16
    return pl.pallas_call(
        functools.partial(scan_kernel, n_layer, n_space, reverse),
        out_shape=jax.ShapeDtypeStruct((n_space * rows, width, channels), jnp.float32),
        in_specs=[pl.BlockSpec(memory_space=pltpu.VMEM)] * 2,
        out_specs=pl.BlockSpec(memory_space=pltpu.VMEM),
        scratch_shapes=[
            pltpu.VMEM((stages, RADIX - 1) + piece, link),
            pltpu.VMEM((n_space - 1,) + piece, link),
            pltpu.VMEM((max(stages - 1, 1),) + piece, link),
            pltpu.VMEM(piece, link),
            pltpu.VMEM(piece, jnp.float32),
            pltpu.SemaphoreType.DMA((stages, RADIX - 1)),
            pltpu.SemaphoreType.DMA((stages, RADIX - 1)),
            pltpu.SemaphoreType.DMA((n_space - 1,)),
            pltpu.SemaphoreType.DMA((n_space - 1,)),
        ],
        compiler_params=pltpu.CompilerParams(
            collective_id=collective_id,
            has_side_effects=True,
            vmem_limit_bytes=8 * 1024 * 1024,
        ),
    )(value.astype(link), base)


def gather_space(piece):
    count = lax.axis_size("space")
    place = lax.axis_index("space")
    rows = piece.shape[0]
    whole = jnp.zeros((count * rows,) + piece.shape[1:], piece.dtype)
    whole = lax.dynamic_update_slice_in_dim(whole, piece, place * rows, 0)
    for shift in range(1, count):
        part = lax.ppermute(
            piece, "space", [(i, (i + shift) % count) for i in range(count)]
        )
        source = (place + count - shift) % count
        whole = lax.dynamic_update_slice_in_dim(whole, part, source * rows, 0)
    return whole


def window_conv(low_window, kernel3, spec):
    height, width, channels = low_window.shape
    out = lax.conv_general_dilated(
        column_chunks(low_window),
        kernel3,
        (1, 1),
        ((0, 0), (0, 0)),
        dimension_numbers=("HNWC", spec, "HNWC"),
        preferred_element_type=jnp.float32,
    )
    return out.reshape(height - 2, width, channels)


def window_rows(whole, rows):
    padded = jnp.pad(whole, ((1, 1), (0, 0), (0, 0)))
    return lax.dynamic_slice_in_dim(padded, lax.axis_index("space") * rows, rows + 2, 0)


def forward_jump(current, kernels, rows):
    start = current
    for kernel3 in kernels[:-1]:
        current = current + step_size * jnp.tanh(conv(current.astype(jnp.bfloat16), kernel3))
    low = window_rows(current.astype(jnp.bfloat16), rows)
    last = own_rows(current, rows) + step_size * jnp.tanh(
        window_conv(low, kernels[-1], "HWIO")
    )
    return last - own_rows(start, rows)


def backward_jump(adjoint, flipped, slopes, rows):
    start = adjoint
    for index in reversed(range(1, len(flipped))):
        scaled = (step_size * slopes[index] * adjoint).astype(jnp.bfloat16)
        adjoint = adjoint + conv_transposed(scaled, flipped[index])
    scaled = (step_size * slopes[0] * adjoint).astype(jnp.bfloat16)
    last = own_rows(adjoint, rows) + window_conv(
        window_rows(scaled, rows), flipped[0], "HWOI"
    )
    return last - own_rows(start, rows)


def own_rows(whole, rows):
    return lax.dynamic_slice_in_dim(whole, lax.axis_index("space") * rows, rows, 0)


def on_device(input_field, weights, cotangent):
    rows = input_field.shape[0]
    channels = weights.shape[3]
    kernels = [w.reshape(3, 3, channels, channels) for w in weights]
    flipped = [k[::-1, ::-1] for k in kernels]
    full_input = gather_space(input_field)
    full_cotangent = gather_space(cotangent)

    begin_state = full_input
    for sweep_index in range(ITERS):
        jump = forward_jump(begin_state, kernels, rows)
        begin_state = scan_and_gather(jump, full_input, False, sweep_index)
    outputs, inputs_low, slopes = forward_block(begin_state, kernels)

    finish = full_cotangent
    for sweep_index in range(ITERS):
        back = backward_jump(finish, flipped, slopes, rows)
        finish = scan_and_gather(back, full_cotangent, True, ITERS + sweep_index)
    begins, scaled_list = backward_block(finish, flipped, slopes)

    quarter = channels // lax.axis_size("space")
    first = lax.axis_index("space") * quarter
    pieces = []
    for low, scaled in zip(inputs_low, scaled_list):
        signal = lax.dynamic_slice_in_dim(scaled, first, quarter, 2)
        grad = kernel_gradient(low, signal)
        pieces.append(jnp.transpose(grad, (3, 1, 2, 0)).reshape(quarter, 9, channels))
    weight_grad = jnp.stack(pieces, axis=1).astype(jnp.bfloat16)
    return (own_rows(outputs, rows)[None], own_rows(begins, rows)[None], weight_grad)


def solution(mesh):
    placed = (P("space", None, None), P("layer", None, None, None), P("space", None, None))
    return jax.shard_map(
        on_device,
        mesh=mesh,
        in_specs=placed,
        out_specs=(
            P("layer", "space", None, None),
            P("layer", "space", None, None),
            P("space", "layer", None, None),
        ),
        check_vma=False,
    )
```

```python
import functools

import jax
import jax.numpy as jnp
from jax import lax
from jax.experimental import pallas as pl
from jax.experimental.pallas import tpu as pltpu
from jax.sharding import PartitionSpec as P

MESH = pl.DeviceIdType.MESH

ITERS = 2
RADIX = 4

step_size = 0.125


CHUNK = 4


def column_chunks(low):
    height, width, channels = low.shape
    padded = jnp.pad(low, ((0, 0), (1, 1), (0, 0)))
    return jnp.stack(
        [padded[:, c : c + CHUNK + 2] for c in range(0, width, CHUNK)], axis=1
    )


def chunked_conv(low, kernel3, spec):
    height, width, channels = low.shape
    out = lax.conv_general_dilated(
        column_chunks(low),
        kernel3,
        (1, 1),
        ((1, 1), (0, 0)),
        dimension_numbers=("HNWC", spec, "HNWC"),
        preferred_element_type=jnp.float32,
    )
    return out.reshape(height, width, kernel3.shape[3] if spec == "HWIO" else kernel3.shape[2])


def conv(low, kernel3):
    return chunked_conv(low, kernel3, "HWIO")


def conv_transposed(low, flipped3):
    return chunked_conv(low, flipped3, "HWOI")


def kernel_gradient(low, signal):
    return lax.conv_general_dilated(
        low[None],
        signal[None],
        (1, 1),
        ((1, 1), (1, 1)),
        dimension_numbers=("CHWN", "IHWO", "NHWC"),
        preferred_element_type=jnp.float32,
    )


def forward_block(current, kernels):
    inputs_low = []
    slopes = []
    for kernel3 in kernels:
        low = current.astype(jnp.bfloat16)
        squashed = jnp.tanh(conv(low, kernel3))
        inputs_low.append(low)
        slopes.append(1.0 - squashed * squashed)
        current = current + step_size * squashed
    return current, inputs_low, slopes


def backward_block(adjoint, flipped, slopes):
    scaled_list = [None] * len(flipped)
    for index in reversed(range(len(flipped))):
        scaled = (step_size * slopes[index] * adjoint).astype(jnp.bfloat16)
        scaled_list[index] = scaled
        adjoint = adjoint + conv_transposed(scaled, flipped[index])
    return adjoint, scaled_list


def shifted_pairs(count, stride, shift):
    pairs = []
    for source in range(count):
        digit = (source // stride) % RADIX
        base = source - digit * stride
        pairs.append((source, base + ((digit + shift) % RADIX) * stride))
    return pairs


def exclusive_scan(value, reverse):
    count = lax.axis_size("layer")
    place = lax.axis_index("layer")
    total = jnp.zeros_like(value)
    stride = 1
    while stride < count:
        digit = (place // stride) % RADIX
        received = [
            lax.ppermute(value, "layer", shifted_pairs(count, stride, shift))
            for shift in range(1, RADIX)
        ]
        group = value
        for shift, part in zip(range(1, RADIX), received):
            earlier = shift > digit if reverse else shift <= digit
            total = total + jnp.where(earlier, part, jnp.zeros_like(part))
            group = group + part
        value = group
        stride *= RADIX
    return total


def scan_kernel(
    n_layer, n_space, reverse, value_ref, base_ref, out_ref,
    slots, gathered, group_buf, mine, total, send_sems, recv_sems, gsend, grecv,
):
    layer = lax.axis_index("layer")
    space = lax.axis_index("space")
    rows = value_ref.shape[0]
    strides = []
    stride = 1
    while stride < n_layer:
        strides.append(stride)
        stride *= RADIX

    partners = []
    for stride in strides:
        digit = (layer // stride) % RADIX
        base = layer - digit * stride
        for shift in range(1, RADIX):
            partners.append((base + ((digit + shift) % RADIX) * stride, space))
    for shift in range(1, n_space):
        partners.append((layer, (space + shift) % n_space))
    barrier = pltpu.get_barrier_semaphore()
    for partner in partners:
        pl.semaphore_signal(barrier, inc=1, device_id=partner, device_id_type=MESH)
    pl.semaphore_wait(barrier, len(partners))

    total[...] = jnp.zeros(total.shape, jnp.float32)
    pending = []
    source = value_ref
    for stage, stride in enumerate(strides):
        last = stage + 1 == len(strides)
        digit = (layer // stride) % RADIX
        base = layer - digit * stride
        copies = []
        for shift in range(1, RADIX):
            copy = pltpu.make_async_remote_copy(
                src_ref=source,
                dst_ref=slots.at[stage, shift - 1],
                send_sem=send_sems.at[stage, shift - 1],
                recv_sem=recv_sems.at[stage, shift - 1],
                device_id=(base + ((digit + shift) % RADIX) * stride, space),
                device_id_type=MESH,
            )
            wraps = digit + shift >= RADIX
            sends = (wraps if reverse else jnp.logical_not(wraps)) if last else None
            gets = (shift > digit if reverse else shift <= digit) if last else None
            copies.append((copy, sends, gets))
            if last:
                pl.when(sends)(copy.start)
            else:
                copy.start()
        for shift, (copy, sends, gets) in zip(range(1, RADIX), copies):
            if last:
                pl.when(gets)(copy.wait_recv)
            else:
                copy.wait_recv()
            pending.append((copy, sends))
        group = source[...].astype(jnp.float32)
        for shift in range(1, RADIX):
            earlier = shift > digit if reverse else shift <= digit

            @pl.when(earlier)
            def _():
                total[...] += slots[stage, shift - 1].astype(jnp.float32)

            if not last:
                group = group + slots[stage, shift - 1].astype(jnp.float32)
        if not last:
            group_buf[stage] = group.astype(group_buf.dtype)
            source = group_buf.at[stage]

    mine[...] = total[...].astype(mine.dtype)
    copies = []
    for shift in range(1, n_space):
        copy = pltpu.make_async_remote_copy(
            src_ref=mine,
            dst_ref=gathered.at[shift - 1],
            send_sem=gsend.at[shift - 1],
            recv_sem=grecv.at[shift - 1],
            device_id=(layer, (space + shift) % n_space),
            device_id_type=MESH,
        )
        copy.start()
        copies.append(copy)
    here = pl.ds(space * rows, rows)
    out_ref[here] = base_ref[here] + total[...]
    for copy in copies:
        copy.wait_recv()
    for shift in range(1, n_space):
        there = pl.ds(((space + n_space - shift) % n_space) * rows, rows)
        out_ref[there] = base_ref[there] + gathered[shift - 1].astype(jnp.float32)
    for copy, sends in pending:
        if sends is None:
            copy.wait_send()
        else:
            pl.when(sends)(copy.wait_send)
    for copy in copies:
        copy.wait_send()


def scan_and_gather(value, base, reverse, collective_id):
    n_layer = lax.axis_size("layer")
    n_space = lax.axis_size("space")
    stages = 0
    while RADIX ** stages < n_layer:
        stages += 1
    assert RADIX ** stages == n_layer
    rows, width, channels = value.shape
    piece = (rows, width, channels)
    link = jnp.bfloat16
    return pl.pallas_call(
        functools.partial(scan_kernel, n_layer, n_space, reverse),
        out_shape=jax.ShapeDtypeStruct((n_space * rows, width, channels), jnp.float32),
        in_specs=[pl.BlockSpec(memory_space=pltpu.VMEM)] * 2,
        out_specs=pl.BlockSpec(memory_space=pltpu.VMEM),
        scratch_shapes=[
            pltpu.VMEM((stages, RADIX - 1) + piece, link),
            pltpu.VMEM((n_space - 1,) + piece, link),
            pltpu.VMEM((max(stages - 1, 1),) + piece, link),
            pltpu.VMEM(piece, link),
            pltpu.VMEM(piece, jnp.float32),
            pltpu.SemaphoreType.DMA((stages, RADIX - 1)),
            pltpu.SemaphoreType.DMA((stages, RADIX - 1)),
            pltpu.SemaphoreType.DMA((n_space - 1,)),
            pltpu.SemaphoreType.DMA((n_space - 1,)),
        ],
        compiler_params=pltpu.CompilerParams(
            collective_id=collective_id,
            has_side_effects=True,
            vmem_limit_bytes=8 * 1024 * 1024,
        ),
    )(value.astype(link), base)


def gather_space(piece):
    count = lax.axis_size("space")
    place = lax.axis_index("space")
    rows = piece.shape[0]
    whole = jnp.zeros((count * rows,) + piece.shape[1:], piece.dtype)
    whole = lax.dynamic_update_slice_in_dim(whole, piece, place * rows, 0)
    for shift in range(1, count):
        part = lax.ppermute(
            piece, "space", [(i, (i + shift) % count) for i in range(count)]
        )
        source = (place + count - shift) % count
        whole = lax.dynamic_update_slice_in_dim(whole, part, source * rows, 0)
    return whole


def window_conv(low_window, kernel3, spec):
    height, width, channels = low_window.shape
    out = lax.conv_general_dilated(
        column_chunks(low_window),
        kernel3,
        (1, 1),
        ((0, 0), (0, 0)),
        dimension_numbers=("HNWC", spec, "HNWC"),
        preferred_element_type=jnp.float32,
    )
    return out.reshape(height - 2, width, channels)


def window_rows(whole, rows):
    padded = jnp.pad(whole, ((1, 1), (0, 0), (0, 0)))
    return lax.dynamic_slice_in_dim(padded, lax.axis_index("space") * rows, rows + 2, 0)


def forward_jump(current, kernels, rows):
    start = current
    for kernel3 in kernels[:-1]:
        current = current + step_size * jnp.tanh(conv(current.astype(jnp.bfloat16), kernel3))
    low = window_rows(current.astype(jnp.bfloat16), rows)
    last = own_rows(current, rows) + step_size * jnp.tanh(
        window_conv(low, kernels[-1], "HWIO")
    )
    return last - own_rows(start, rows)


def own_rows(whole, rows):
    return lax.dynamic_slice_in_dim(whole, lax.axis_index("space") * rows, rows, 0)


def on_device(input_field, weights, cotangent):
    rows = input_field.shape[0]
    channels = weights.shape[3]
    kernels = [w.reshape(3, 3, channels, channels) for w in weights]
    flipped = [k[::-1, ::-1] for k in kernels]
    full_input = gather_space(input_field)
    full_cotangent = gather_space(cotangent)

    begin_state = full_input
    for sweep_index in range(ITERS):
        jump = forward_jump(begin_state, kernels, rows)
        begin_state = scan_and_gather(jump, full_input, False, sweep_index)
    outputs, inputs_low, slopes = forward_block(begin_state, kernels)

    finish = full_cotangent
    for sweep_index in range(ITERS):
        begins, _ = backward_block(finish, flipped, slopes)
        back = own_rows(begins - finish, rows)
        finish = scan_and_gather(back, full_cotangent, True, ITERS + sweep_index)
    begins, scaled_list = backward_block(finish, flipped, slopes)

    quarter = channels // lax.axis_size("space")
    first = lax.axis_index("space") * quarter
    pieces = []
    for low, scaled in zip(inputs_low, scaled_list):
        signal = lax.dynamic_slice_in_dim(scaled, first, quarter, 2)
        grad = kernel_gradient(low, signal)
        pieces.append(jnp.transpose(grad, (3, 1, 2, 0)).reshape(quarter, 9, channels))
    weight_grad = jnp.stack(pieces, axis=1).astype(jnp.bfloat16)
    return (own_rows(outputs, rows)[None], own_rows(begins, rows)[None], weight_grad)


def solution(mesh):
    placed = (P("space", None, None), P("layer", None, None, None), P("space", None, None))
    return jax.shard_map(
        on_device,
        mesh=mesh,
        in_specs=placed,
        out_specs=(
            P("layer", "space", None, None),
            P("layer", "space", None, None),
            P("space", "layer", None, None),
        ),
        check_vma=False,
    )
```

```python
import functools

import jax
import jax.numpy as jnp
from jax import lax
from jax.experimental import pallas as pl
from jax.experimental.pallas import tpu as pltpu
from jax.sharding import PartitionSpec as P

MESH = pl.DeviceIdType.MESH

ITERS = 2
RADIX = 4

step_size = 0.125


CHUNK = 4


def column_chunks(low):
    height, width, channels = low.shape
    padded = jnp.pad(low, ((0, 0), (1, 1), (0, 0)))
    return jnp.stack(
        [padded[:, c : c + CHUNK + 2] for c in range(0, width, CHUNK)], axis=1
    )


def chunked_conv(low, kernel3, spec):
    height, width, channels = low.shape
    out = lax.conv_general_dilated(
        column_chunks(low),
        kernel3,
        (1, 1),
        ((1, 1), (0, 0)),
        dimension_numbers=("HNWC", spec, "HNWC"),
        preferred_element_type=jnp.float32,
    )
    return out.reshape(height, width, kernel3.shape[3] if spec == "HWIO" else kernel3.shape[2])


def conv(low, kernel3):
    return chunked_conv(low, kernel3, "HWIO")


def conv_transposed(low, flipped3):
    return chunked_conv(low, flipped3, "HWOI")


def kernel_gradient(low, signal):
    return lax.conv_general_dilated(
        low[None],
        signal[None],
        (1, 1),
        ((1, 1), (1, 1)),
        dimension_numbers=("CHWN", "IHWO", "NHWC"),
        preferred_element_type=jnp.float32,
    )


def forward_block(current, kernels):
    inputs_low = []
    slopes = []
    for kernel3 in kernels:
        low = current.astype(jnp.bfloat16)
        squashed = jnp.tanh(conv(low, kernel3))
        inputs_low.append(low)
        slopes.append(1.0 - squashed * squashed)
        current = current + step_size * squashed
    return current, inputs_low, slopes


def backward_block(adjoint, flipped, slopes):
    scaled_list = [None] * len(flipped)
    for index in reversed(range(len(flipped))):
        scaled = (step_size * slopes[index] * adjoint).astype(jnp.bfloat16)
        scaled_list[index] = scaled
        adjoint = adjoint + conv_transposed(scaled, flipped[index])
    return adjoint, scaled_list


def shifted_pairs(count, stride, shift):
    pairs = []
    for source in range(count):
        digit = (source // stride) % RADIX
        base = source - digit * stride
        pairs.append((source, base + ((digit + shift) % RADIX) * stride))
    return pairs


def exclusive_scan(value, reverse):
    count = lax.axis_size("layer")
    place = lax.axis_index("layer")
    total = jnp.zeros_like(value)
    stride = 1
    while stride < count:
        digit = (place // stride) % RADIX
        received = [
            lax.ppermute(value, "layer", shifted_pairs(count, stride, shift))
            for shift in range(1, RADIX)
        ]
        group = value
        for shift, part in zip(range(1, RADIX), received):
            earlier = shift > digit if reverse else shift <= digit
            total = total + jnp.where(earlier, part, jnp.zeros_like(part))
            group = group + part
        value = group
        stride *= RADIX
    return total


def scan_kernel(
    n_layer, n_space, reverse, value_ref, base_ref, out_ref,
    slots, gathered, group_buf, mine, total, send_sems, recv_sems, gsend, grecv,
):
    layer = lax.axis_index("layer")
    space = lax.axis_index("space")
    rows = value_ref.shape[0]
    strides = []
    stride = 1
    while stride < n_layer:
        strides.append(stride)
        stride *= RADIX

    partners = []
    for stride in strides:
        digit = (layer // stride) % RADIX
        base = layer - digit * stride
        for shift in range(1, RADIX):
            partners.append((base + ((digit + shift) % RADIX) * stride, space))
    for shift in range(1, n_space):
        partners.append((layer, (space + shift) % n_space))
    barrier = pltpu.get_barrier_semaphore()
    for partner in partners:
        pl.semaphore_signal(barrier, inc=1, device_id=partner, device_id_type=MESH)
    pl.semaphore_wait(barrier, len(partners))

    total[...] = jnp.zeros(total.shape, jnp.float32)
    pending = []
    source = value_ref
    for stage, stride in enumerate(strides):
        last = stage + 1 == len(strides)
        digit = (layer // stride) % RADIX
        base = layer - digit * stride
        copies = []
        for shift in range(1, RADIX):
            copy = pltpu.make_async_remote_copy(
                src_ref=source,
                dst_ref=slots.at[stage, shift - 1],
                send_sem=send_sems.at[stage, shift - 1],
                recv_sem=recv_sems.at[stage, shift - 1],
                device_id=(base + ((digit + shift) % RADIX) * stride, space),
                device_id_type=MESH,
            )
            wraps = digit + shift >= RADIX
            sends = (wraps if reverse else jnp.logical_not(wraps)) if last else None
            gets = (shift > digit if reverse else shift <= digit) if last else None
            copies.append((copy, sends, gets))
            if last:
                pl.when(sends)(copy.start)
            else:
                copy.start()
        for shift, (copy, sends, gets) in zip(range(1, RADIX), copies):
            if last:
                pl.when(gets)(copy.wait_recv)
            else:
                copy.wait_recv()
            pending.append((copy, sends))
        group = source[...].astype(jnp.float32)
        for shift in range(1, RADIX):
            earlier = shift > digit if reverse else shift <= digit

            @pl.when(earlier)
            def _():
                total[...] += slots[stage, shift - 1].astype(jnp.float32)

            if not last:
                group = group + slots[stage, shift - 1].astype(jnp.float32)
        if not last:
            group_buf[stage] = group.astype(group_buf.dtype)
            source = group_buf.at[stage]

    mine[...] = total[...].astype(mine.dtype)
    copies = []
    for shift in range(1, n_space):
        copy = pltpu.make_async_remote_copy(
            src_ref=mine,
            dst_ref=gathered.at[shift - 1],
            send_sem=gsend.at[shift - 1],
            recv_sem=grecv.at[shift - 1],
            device_id=(layer, (space + shift) % n_space),
            device_id_type=MESH,
        )
        copy.start()
        copies.append(copy)
    here = pl.ds(space * rows, rows)
    out_ref[here] = base_ref[here] + total[...]
    for copy in copies:
        copy.wait_recv()
    for shift in range(1, n_space):
        there = pl.ds(((space + n_space - shift) % n_space) * rows, rows)
        out_ref[there] = base_ref[there] + gathered[shift - 1].astype(jnp.float32)
    for copy, sends in pending:
        if sends is None:
            copy.wait_send()
        else:
            pl.when(sends)(copy.wait_send)
    for copy in copies:
        copy.wait_send()


def scan_and_gather(value, base, reverse, collective_id):
    n_layer = lax.axis_size("layer")
    n_space = lax.axis_size("space")
    stages = 0
    while RADIX ** stages < n_layer:
        stages += 1
    assert RADIX ** stages == n_layer
    rows, width, channels = value.shape
    piece = (rows, width, channels)
    link = jnp.bfloat16
    return pl.pallas_call(
        functools.partial(scan_kernel, n_layer, n_space, reverse),
        out_shape=jax.ShapeDtypeStruct((n_space * rows, width, channels), jnp.float32),
        in_specs=[pl.BlockSpec(memory_space=pltpu.VMEM)] * 2,
        out_specs=pl.BlockSpec(memory_space=pltpu.VMEM),
        scratch_shapes=[
            pltpu.VMEM((stages, RADIX - 1) + piece, link),
            pltpu.VMEM((n_space - 1,) + piece, link),
            pltpu.VMEM((max(stages - 1, 1),) + piece, link),
            pltpu.VMEM(piece, link),
            pltpu.VMEM(piece, jnp.float32),
            pltpu.SemaphoreType.DMA((stages, RADIX - 1)),
            pltpu.SemaphoreType.DMA((stages, RADIX - 1)),
            pltpu.SemaphoreType.DMA((n_space - 1,)),
            pltpu.SemaphoreType.DMA((n_space - 1,)),
        ],
        compiler_params=pltpu.CompilerParams(
            collective_id=collective_id,
            has_side_effects=True,
            vmem_limit_bytes=8 * 1024 * 1024,
        ),
    )(value.astype(link), base)


def gather_space(piece):
    count = lax.axis_size("space")
    place = lax.axis_index("space")
    rows = piece.shape[0]
    whole = jnp.zeros((count * rows,) + piece.shape[1:], piece.dtype)
    whole = lax.dynamic_update_slice_in_dim(whole, piece, place * rows, 0)
    for shift in range(1, count):
        part = lax.ppermute(
            piece, "space", [(i, (i + shift) % count) for i in range(count)]
        )
        source = (place + count - shift) % count
        whole = lax.dynamic_update_slice_in_dim(whole, part, source * rows, 0)
    return whole


def window_conv(low_window, kernel3, spec):
    height, width, channels = low_window.shape
    out = lax.conv_general_dilated(
        column_chunks(low_window),
        kernel3,
        (1, 1),
        ((0, 0), (0, 0)),
        dimension_numbers=("HNWC", spec, "HNWC"),
        preferred_element_type=jnp.float32,
    )
    return out.reshape(height - 2, width, channels)


def window_rows(whole, rows):
    padded = jnp.pad(whole, ((1, 1), (0, 0), (0, 0)))
    return lax.dynamic_slice_in_dim(padded, lax.axis_index("space") * rows, rows + 2, 0)


def forward_jump(current, kernels, rows):
    halo = len(kernels)
    height = current.shape[0]
    first = lax.axis_index("space") * rows
    padded = jnp.pad(current, ((halo, halo), (0, 0), (0, 0)))
    window = lax.dynamic_slice_in_dim(padded, first, rows + 2 * halo, 0)
    index = first - halo + jnp.arange(rows + 2 * halo)
    inside = ((index >= 0) & (index < height))[:, None, None]
    for kernel3 in kernels:
        low = jnp.where(inside, window, jnp.zeros_like(window)).astype(jnp.bfloat16)
        window = window[1:-1] + step_size * jnp.tanh(window_conv(low, kernel3, "HWIO"))
        inside = inside[1:-1]
    return window - own_rows(current, rows)


def own_rows(whole, rows):
    return lax.dynamic_slice_in_dim(whole, lax.axis_index("space") * rows, rows, 0)


def on_device(input_field, weights, cotangent):
    rows = input_field.shape[0]
    channels = weights.shape[3]
    kernels = [w.reshape(3, 3, channels, channels) for w in weights]
    flipped = [k[::-1, ::-1] for k in kernels]
    full_input = gather_space(input_field)
    full_cotangent = gather_space(cotangent)

    begin_state = full_input
    for sweep_index in range(ITERS):
        jump = forward_jump(begin_state, kernels, rows)
        begin_state = scan_and_gather(jump, full_input, False, sweep_index)
    outputs, inputs_low, slopes = forward_block(begin_state, kernels)

    finish = full_cotangent
    for sweep_index in range(ITERS):
        begins, _ = backward_block(finish, flipped, slopes)
        back = own_rows(begins - finish, rows)
        finish = scan_and_gather(back, full_cotangent, True, ITERS + sweep_index)
    begins, scaled_list = backward_block(finish, flipped, slopes)

    quarter = channels // lax.axis_size("space")
    first = lax.axis_index("space") * quarter
    pieces = []
    for low, scaled in zip(inputs_low, scaled_list):
        signal = lax.dynamic_slice_in_dim(scaled, first, quarter, 2)
        grad = kernel_gradient(low, signal)
        pieces.append(jnp.transpose(grad, (3, 1, 2, 0)).reshape(quarter, 9, channels))
    weight_grad = jnp.stack(pieces, axis=1).astype(jnp.bfloat16)
    return (own_rows(outputs, rows)[None], own_rows(begins, rows)[None], weight_grad)


def solution(mesh):
    placed = (P("space", None, None), P("layer", None, None, None), P("space", None, None))
    return jax.shard_map(
        on_device,
        mesh=mesh,
        in_specs=placed,
        out_specs=(
            P("layer", "space", None, None),
            P("layer", "space", None, None),
            P("space", "layer", None, None),
        ),
        check_vma=False,
    )
```

```python
import functools

import jax
import jax.numpy as jnp
from jax import lax
from jax.experimental import pallas as pl
from jax.experimental.pallas import tpu as pltpu
from jax.sharding import PartitionSpec as P

MESH = pl.DeviceIdType.MESH

ITERS = 2
RADIX = 4

step_size = 0.125


CHUNK = 4


def column_chunks(low):
    height, width, channels = low.shape
    padded = jnp.pad(low, ((0, 0), (1, 1), (0, 0)))
    return jnp.stack(
        [padded[:, c : c + CHUNK + 2] for c in range(0, width, CHUNK)], axis=1
    )


def chunked_conv(low, kernel3, spec):
    height, width, channels = low.shape
    out = lax.conv_general_dilated(
        column_chunks(low),
        kernel3,
        (1, 1),
        ((1, 1), (0, 0)),
        dimension_numbers=("HNWC", spec, "HNWC"),
        preferred_element_type=jnp.float32,
    )
    return out.reshape(height, width, kernel3.shape[3] if spec == "HWIO" else kernel3.shape[2])


def conv(low, kernel3):
    return chunked_conv(low, kernel3, "HWIO")


def conv_transposed(low, flipped3):
    return chunked_conv(low, flipped3, "HWOI")


def kernel_gradient(low, signal):
    return lax.conv_general_dilated(
        low[None],
        signal[None],
        (1, 1),
        ((1, 1), (1, 1)),
        dimension_numbers=("CHWN", "IHWO", "NHWC"),
        preferred_element_type=jnp.float32,
    )


def forward_block(current, kernels):
    inputs_low = []
    slopes = []
    for kernel3 in kernels:
        low = current.astype(jnp.bfloat16)
        squashed = jnp.tanh(conv(low, kernel3))
        inputs_low.append(low)
        slopes.append(1.0 - squashed * squashed)
        current = current + step_size * squashed
    return current, inputs_low, slopes


def backward_block(adjoint, flipped, slopes):
    scaled_list = [None] * len(flipped)
    for index in reversed(range(len(flipped))):
        scaled = (step_size * slopes[index] * adjoint).astype(jnp.bfloat16)
        scaled_list[index] = scaled
        adjoint = adjoint + conv_transposed(scaled, flipped[index])
    return adjoint, scaled_list


def shifted_pairs(count, stride, shift):
    pairs = []
    for source in range(count):
        digit = (source // stride) % RADIX
        base = source - digit * stride
        pairs.append((source, base + ((digit + shift) % RADIX) * stride))
    return pairs


def exclusive_scan(value, reverse):
    count = lax.axis_size("layer")
    place = lax.axis_index("layer")
    total = jnp.zeros_like(value)
    stride = 1
    while stride < count:
        digit = (place // stride) % RADIX
        received = [
            lax.ppermute(value, "layer", shifted_pairs(count, stride, shift))
            for shift in range(1, RADIX)
        ]
        group = value
        for shift, part in zip(range(1, RADIX), received):
            earlier = shift > digit if reverse else shift <= digit
            total = total + jnp.where(earlier, part, jnp.zeros_like(part))
            group = group + part
        value = group
        stride *= RADIX
    return total


def scan_kernel(
    n_layer, n_space, reverse, value_ref, base_ref, out_ref,
    slots, gathered, group_buf, mine, total, send_sems, recv_sems, gsend, grecv,
):
    layer = lax.axis_index("layer")
    space = lax.axis_index("space")
    rows = value_ref.shape[0]
    strides = []
    stride = 1
    while stride < n_layer:
        strides.append(stride)
        stride *= RADIX

    partners = []
    for stride in strides:
        digit = (layer // stride) % RADIX
        base = layer - digit * stride
        for shift in range(1, RADIX):
            partners.append((base + ((digit + shift) % RADIX) * stride, space))
    for shift in range(1, n_space):
        partners.append((layer, (space + shift) % n_space))
    barrier = pltpu.get_barrier_semaphore()
    for partner in partners:
        pl.semaphore_signal(barrier, inc=1, device_id=partner, device_id_type=MESH)
    pl.semaphore_wait(barrier, len(partners))

    total[...] = jnp.zeros(total.shape, jnp.float32)
    pending = []
    source = value_ref
    for stage, stride in enumerate(strides):
        last = stage + 1 == len(strides)
        digit = (layer // stride) % RADIX
        base = layer - digit * stride
        copies = []
        for shift in range(1, RADIX):
            copy = pltpu.make_async_remote_copy(
                src_ref=source,
                dst_ref=slots.at[stage, shift - 1],
                send_sem=send_sems.at[stage, shift - 1],
                recv_sem=recv_sems.at[stage, shift - 1],
                device_id=(base + ((digit + shift) % RADIX) * stride, space),
                device_id_type=MESH,
            )
            wraps = digit + shift >= RADIX
            sends = (wraps if reverse else jnp.logical_not(wraps)) if last else None
            gets = (shift > digit if reverse else shift <= digit) if last else None
            copies.append((copy, sends, gets))
            if last:
                pl.when(sends)(copy.start)
            else:
                copy.start()
        for shift, (copy, sends, gets) in zip(range(1, RADIX), copies):
            if last:
                pl.when(gets)(copy.wait_recv)
            else:
                copy.wait_recv()
            pending.append((copy, sends))
        group = source[...].astype(jnp.float32)
        for shift in range(1, RADIX):
            earlier = shift > digit if reverse else shift <= digit

            @pl.when(earlier)
            def _():
                total[...] += slots[stage, shift - 1].astype(jnp.float32)

            if not last:
                group = group + slots[stage, shift - 1].astype(jnp.float32)
        if not last:
            group_buf[stage] = group.astype(group_buf.dtype)
            source = group_buf.at[stage]

    mine[...] = total[...].astype(mine.dtype)
    copies = []
    for shift in range(1, n_space):
        copy = pltpu.make_async_remote_copy(
            src_ref=mine,
            dst_ref=gathered.at[shift - 1],
            send_sem=gsend.at[shift - 1],
            recv_sem=grecv.at[shift - 1],
            device_id=(layer, (space + shift) % n_space),
            device_id_type=MESH,
        )
        copy.start()
        copies.append(copy)
    here = pl.ds(space * rows, rows)
    out_ref[here] = base_ref[here] + total[...]
    for copy in copies:
        copy.wait_recv()
    for shift in range(1, n_space):
        there = pl.ds(((space + n_space - shift) % n_space) * rows, rows)
        out_ref[there] = base_ref[there] + gathered[shift - 1].astype(jnp.float32)
    for copy, sends in pending:
        if sends is None:
            copy.wait_send()
        else:
            pl.when(sends)(copy.wait_send)
    for copy in copies:
        copy.wait_send()


def scan_and_gather(value, base, reverse, collective_id):
    n_layer = lax.axis_size("layer")
    n_space = lax.axis_size("space")
    stages = 0
    while RADIX ** stages < n_layer:
        stages += 1
    assert RADIX ** stages == n_layer
    rows, width, channels = value.shape
    piece = (rows, width, channels)
    link = jnp.bfloat16
    return pl.pallas_call(
        functools.partial(scan_kernel, n_layer, n_space, reverse),
        out_shape=jax.ShapeDtypeStruct((n_space * rows, width, channels), jnp.float32),
        in_specs=[pl.BlockSpec(memory_space=pltpu.VMEM)] * 2,
        out_specs=pl.BlockSpec(memory_space=pltpu.VMEM),
        scratch_shapes=[
            pltpu.VMEM((stages, RADIX - 1) + piece, link),
            pltpu.VMEM((n_space - 1,) + piece, link),
            pltpu.VMEM((max(stages - 1, 1),) + piece, link),
            pltpu.VMEM(piece, link),
            pltpu.VMEM(piece, jnp.float32),
            pltpu.SemaphoreType.DMA((stages, RADIX - 1)),
            pltpu.SemaphoreType.DMA((stages, RADIX - 1)),
            pltpu.SemaphoreType.DMA((n_space - 1,)),
            pltpu.SemaphoreType.DMA((n_space - 1,)),
        ],
        compiler_params=pltpu.CompilerParams(
            collective_id=collective_id,
            has_side_effects=True,
            vmem_limit_bytes=8 * 1024 * 1024,
        ),
    )(value.astype(link), base)


def gather_space(piece):
    count = lax.axis_size("space")
    place = lax.axis_index("space")
    rows = piece.shape[0]
    whole = jnp.zeros((count * rows,) + piece.shape[1:], piece.dtype)
    whole = lax.dynamic_update_slice_in_dim(whole, piece, place * rows, 0)
    for shift in range(1, count):
        part = lax.ppermute(
            piece, "space", [(i, (i + shift) % count) for i in range(count)]
        )
        source = (place + count - shift) % count
        whole = lax.dynamic_update_slice_in_dim(whole, part, source * rows, 0)
    return whole


def window_conv(low_window, kernel3, spec):
    height, width, channels = low_window.shape
    out = lax.conv_general_dilated(
        column_chunks(low_window),
        kernel3,
        (1, 1),
        ((0, 0), (0, 0)),
        dimension_numbers=("HNWC", spec, "HNWC"),
        preferred_element_type=jnp.float32,
    )
    return out.reshape(height - 2, width, channels)


def window_rows(whole, rows):
    padded = jnp.pad(whole, ((1, 1), (0, 0), (0, 0)))
    return lax.dynamic_slice_in_dim(padded, lax.axis_index("space") * rows, rows + 2, 0)


def forward_jump(current, kernels, rows):
    start = current
    for kernel3 in kernels[:-1]:
        current = current + step_size * jnp.tanh(conv(current.astype(jnp.bfloat16), kernel3))
    low = window_rows(current.astype(jnp.bfloat16), rows)
    last = own_rows(current, rows) + step_size * jnp.tanh(
        window_conv(low, kernels[-1], "HWIO")
    )
    return last - own_rows(start, rows)


def backward_jump(adjoint, flipped, slopes, rows):
    start = adjoint
    for index in reversed(range(1, len(flipped))):
        scaled = (step_size * slopes[index] * adjoint).astype(jnp.bfloat16)
        adjoint = adjoint + conv_transposed(scaled, flipped[index])
    window = window_rows(step_size * slopes[0] * adjoint, rows).astype(jnp.bfloat16)
    last = own_rows(adjoint, rows) + window_conv(window, flipped[0], "HWOI")
    return last - own_rows(start, rows)


def own_rows(whole, rows):
    return lax.dynamic_slice_in_dim(whole, lax.axis_index("space") * rows, rows, 0)


def on_device(input_field, weights, cotangent):
    rows = input_field.shape[0]
    channels = weights.shape[3]
    kernels = [w.reshape(3, 3, channels, channels) for w in weights]
    flipped = [k[::-1, ::-1] for k in kernels]
    full_input = gather_space(input_field)
    full_cotangent = gather_space(cotangent)

    begin_state = full_input
    for sweep_index in range(ITERS):
        jump = forward_jump(begin_state, kernels, rows)
        begin_state = scan_and_gather(jump, full_input, False, sweep_index)
    outputs, inputs_low, slopes = forward_block(begin_state, kernels)

    finish = full_cotangent
    for sweep_index in range(ITERS):
        back = backward_jump(finish, flipped, slopes, rows)
        finish = scan_and_gather(back, full_cotangent, True, ITERS + sweep_index)
    begins, scaled_list = backward_block(finish, flipped, slopes)

    quarter = channels // lax.axis_size("space")
    first = lax.axis_index("space") * quarter
    pieces = []
    for low, scaled in zip(inputs_low, scaled_list):
        signal = lax.dynamic_slice_in_dim(scaled, first, quarter, 2)
        grad = kernel_gradient(low, signal)
        pieces.append(jnp.transpose(grad, (3, 1, 2, 0)).reshape(quarter, 9, channels))
    weight_grad = jnp.stack(pieces, axis=1).astype(jnp.bfloat16)
    return (own_rows(outputs, rows)[None], own_rows(begins, rows)[None], weight_grad)


def solution(mesh):
    placed = (P("space", None, None), P("layer", None, None, None), P("space", None, None))
    return jax.shard_map(
        on_device,
        mesh=mesh,
        in_specs=placed,
        out_specs=(
            P("layer", "space", None, None),
            P("layer", "space", None, None),
            P("space", "layer", None, None),
        ),
        check_vma=False,
    )
```

```python
import functools

import jax
import jax.numpy as jnp
from jax import lax
from jax.experimental import pallas as pl
from jax.experimental.pallas import tpu as pltpu
from jax.sharding import PartitionSpec as P

MESH = pl.DeviceIdType.MESH

ITERS = 2
RADIX = 4

step_size = 0.125


CHUNK = 4


def column_chunks(low):
    height, width, channels = low.shape
    padded = jnp.pad(low, ((0, 0), (1, 1), (0, 0)))
    return jnp.stack(
        [padded[:, c : c + CHUNK + 2] for c in range(0, width, CHUNK)], axis=1
    )


def chunked_conv(low, kernel3, spec):
    height, width, channels = low.shape
    out = lax.conv_general_dilated(
        column_chunks(low),
        kernel3,
        (1, 1),
        ((1, 1), (0, 0)),
        dimension_numbers=("HNWC", spec, "HNWC"),
        preferred_element_type=jnp.float32,
    )
    return out.reshape(height, width, kernel3.shape[3] if spec == "HWIO" else kernel3.shape[2])


def conv(low, kernel3):
    return chunked_conv(low, kernel3, "HWIO")


def conv_transposed(low, flipped3):
    return chunked_conv(low, flipped3, "HWOI")


def kernel_gradient(low, signal):
    return lax.conv_general_dilated(
        low[None],
        signal[None],
        (1, 1),
        ((1, 1), (1, 1)),
        dimension_numbers=("CHWN", "IHWO", "NHWC"),
        preferred_element_type=jnp.float32,
    )


def forward_block(current, kernels):
    inputs_low = []
    slopes = []
    for kernel3 in kernels:
        low = current.astype(jnp.bfloat16)
        squashed = jnp.tanh(conv(low, kernel3))
        inputs_low.append(low)
        slopes.append(1.0 - squashed * squashed)
        current = current + step_size * squashed
    return current, inputs_low, slopes


def backward_block(adjoint, flipped, slopes):
    scaled_list = [None] * len(flipped)
    for index in reversed(range(len(flipped))):
        scaled = (step_size * slopes[index] * adjoint).astype(jnp.bfloat16)
        scaled_list[index] = scaled
        adjoint = adjoint + conv_transposed(scaled, flipped[index])
    return adjoint, scaled_list


def shifted_pairs(count, stride, shift):
    pairs = []
    for source in range(count):
        digit = (source // stride) % RADIX
        base = source - digit * stride
        pairs.append((source, base + ((digit + shift) % RADIX) * stride))
    return pairs


def exclusive_scan(value, reverse):
    count = lax.axis_size("layer")
    place = lax.axis_index("layer")
    total = jnp.zeros_like(value)
    stride = 1
    while stride < count:
        digit = (place // stride) % RADIX
        received = [
            lax.ppermute(value, "layer", shifted_pairs(count, stride, shift))
            for shift in range(1, RADIX)
        ]
        group = value
        for shift, part in zip(range(1, RADIX), received):
            earlier = shift > digit if reverse else shift <= digit
            total = total + jnp.where(earlier, part, jnp.zeros_like(part))
            group = group + part
        value = group
        stride *= RADIX
    return total


def scan_kernel(
    n_layer, n_space, reverse, value_ref, base_ref, out_ref,
    slots, gathered, group_buf, mine, total, send_sems, recv_sems, gsend, grecv,
):
    layer = lax.axis_index("layer")
    space = lax.axis_index("space")
    rows = value_ref.shape[0]
    strides = []
    stride = 1
    while stride < n_layer:
        strides.append(stride)
        stride *= RADIX

    partners = []
    for stride in strides:
        digit = (layer // stride) % RADIX
        base = layer - digit * stride
        for shift in range(1, RADIX):
            partners.append((base + ((digit + shift) % RADIX) * stride, space))
    for shift in range(1, n_space):
        partners.append((layer, (space + shift) % n_space))
    barrier = pltpu.get_barrier_semaphore()
    for partner in partners:
        pl.semaphore_signal(barrier, inc=1, device_id=partner, device_id_type=MESH)
    pl.semaphore_wait(barrier, len(partners))

    total[...] = jnp.zeros(total.shape, jnp.float32)
    pending = []
    source = value_ref
    for stage, stride in enumerate(strides):
        last = stage + 1 == len(strides)
        digit = (layer // stride) % RADIX
        base = layer - digit * stride
        copies = []
        for shift in range(1, RADIX):
            copy = pltpu.make_async_remote_copy(
                src_ref=source,
                dst_ref=slots.at[stage, shift - 1],
                send_sem=send_sems.at[stage, shift - 1],
                recv_sem=recv_sems.at[stage, shift - 1],
                device_id=(base + ((digit + shift) % RADIX) * stride, space),
                device_id_type=MESH,
            )
            wraps = digit + shift >= RADIX
            sends = (wraps if reverse else jnp.logical_not(wraps)) if last else None
            gets = (shift > digit if reverse else shift <= digit) if last else None
            copies.append((copy, sends, gets))
            if last:
                pl.when(sends)(copy.start)
            else:
                copy.start()
        for shift, (copy, sends, gets) in zip(range(1, RADIX), copies):
            if last:
                pl.when(gets)(copy.wait_recv)
            else:
                copy.wait_recv()
            pending.append((copy, sends))
        group = source[...].astype(jnp.float32)
        for shift in range(1, RADIX):
            earlier = shift > digit if reverse else shift <= digit

            @pl.when(earlier)
            def _():
                total[...] += slots[stage, shift - 1].astype(jnp.float32)

            if not last:
                group = group + slots[stage, shift - 1].astype(jnp.float32)
        if not last:
            group_buf[stage] = group.astype(group_buf.dtype)
            source = group_buf.at[stage]

    mine[...] = total[...].astype(mine.dtype)
    copies = []
    for shift in range(1, n_space):
        copy = pltpu.make_async_remote_copy(
            src_ref=mine,
            dst_ref=gathered.at[shift - 1],
            send_sem=gsend.at[shift - 1],
            recv_sem=grecv.at[shift - 1],
            device_id=(layer, (space + shift) % n_space),
            device_id_type=MESH,
        )
        copy.start()
        copies.append(copy)
    here = pl.ds(space * rows, rows)
    out_ref[here] = base_ref[here] + total[...]
    for copy in copies:
        copy.wait_recv()
    for shift in range(1, n_space):
        there = pl.ds(((space + n_space - shift) % n_space) * rows, rows)
        out_ref[there] = base_ref[there] + gathered[shift - 1].astype(jnp.float32)
    for copy, sends in pending:
        if sends is None:
            copy.wait_send()
        else:
            pl.when(sends)(copy.wait_send)
    for copy in copies:
        copy.wait_send()


def scan_and_gather(value, base, reverse, collective_id):
    n_layer = lax.axis_size("layer")
    n_space = lax.axis_size("space")
    stages = 0
    while RADIX ** stages < n_layer:
        stages += 1
    assert RADIX ** stages == n_layer
    rows, width, channels = value.shape
    piece = (rows, width, channels)
    link = jnp.bfloat16
    return pl.pallas_call(
        functools.partial(scan_kernel, n_layer, n_space, reverse),
        out_shape=jax.ShapeDtypeStruct((n_space * rows, width, channels), jnp.float32),
        in_specs=[pl.BlockSpec(memory_space=pltpu.VMEM)] * 2,
        out_specs=pl.BlockSpec(memory_space=pltpu.VMEM),
        scratch_shapes=[
            pltpu.VMEM((stages, RADIX - 1) + piece, link),
            pltpu.VMEM((n_space - 1,) + piece, link),
            pltpu.VMEM((max(stages - 1, 1),) + piece, link),
            pltpu.VMEM(piece, link),
            pltpu.VMEM(piece, jnp.float32),
            pltpu.SemaphoreType.DMA((stages, RADIX - 1)),
            pltpu.SemaphoreType.DMA((stages, RADIX - 1)),
            pltpu.SemaphoreType.DMA((n_space - 1,)),
            pltpu.SemaphoreType.DMA((n_space - 1,)),
        ],
        compiler_params=pltpu.CompilerParams(
            collective_id=collective_id,
            has_side_effects=True,
        ),
    )(value.astype(link), base)


def gather_space(piece):
    count = lax.axis_size("space")
    place = lax.axis_index("space")
    rows = piece.shape[0]
    whole = jnp.zeros((count * rows,) + piece.shape[1:], piece.dtype)
    whole = lax.dynamic_update_slice_in_dim(whole, piece, place * rows, 0)
    for shift in range(1, count):
        part = lax.ppermute(
            piece, "space", [(i, (i + shift) % count) for i in range(count)]
        )
        source = (place + count - shift) % count
        whole = lax.dynamic_update_slice_in_dim(whole, part, source * rows, 0)
    return whole


def window_conv(low_window, kernel3, spec):
    height, width, channels = low_window.shape
    out = lax.conv_general_dilated(
        column_chunks(low_window),
        kernel3,
        (1, 1),
        ((0, 0), (0, 0)),
        dimension_numbers=("HNWC", spec, "HNWC"),
        preferred_element_type=jnp.float32,
    )
    return out.reshape(height - 2, width, channels)


def window_rows(whole, rows):
    padded = jnp.pad(whole, ((1, 1), (0, 0), (0, 0)))
    return lax.dynamic_slice_in_dim(padded, lax.axis_index("space") * rows, rows + 2, 0)


def forward_jump(current, kernels, rows):
    start = current
    for kernel3 in kernels[:-1]:
        current = current + step_size * jnp.tanh(conv(current.astype(jnp.bfloat16), kernel3))
    low = window_rows(current.astype(jnp.bfloat16), rows)
    last = own_rows(current, rows) + step_size * jnp.tanh(
        window_conv(low, kernels[-1], "HWIO")
    )
    return last - own_rows(start, rows)


def own_rows(whole, rows):
    return lax.dynamic_slice_in_dim(whole, lax.axis_index("space") * rows, rows, 0)


def on_device(input_field, weights, cotangent):
    rows = input_field.shape[0]
    channels = weights.shape[3]
    kernels = [w.reshape(3, 3, channels, channels) for w in weights]
    flipped = [k[::-1, ::-1] for k in kernels]
    full_input = gather_space(input_field)
    full_cotangent = gather_space(cotangent)

    begin_state = full_input
    for sweep_index in range(ITERS):
        jump = forward_jump(begin_state, kernels, rows)
        begin_state = scan_and_gather(jump, full_input, False, sweep_index)
    outputs, inputs_low, slopes = forward_block(begin_state, kernels)

    finish = full_cotangent
    for sweep_index in range(ITERS):
        begins, _ = backward_block(finish, flipped, slopes)
        back = own_rows(begins - finish, rows)
        finish = scan_and_gather(back, full_cotangent, True, ITERS + sweep_index)
    begins, scaled_list = backward_block(finish, flipped, slopes)

    quarter = channels // lax.axis_size("space")
    first = lax.axis_index("space") * quarter
    pieces = []
    for low, scaled in zip(inputs_low, scaled_list):
        signal = lax.dynamic_slice_in_dim(scaled, first, quarter, 2)
        grad = kernel_gradient(low, signal)
        pieces.append(jnp.transpose(grad, (3, 1, 2, 0)).reshape(quarter, 9, channels))
    weight_grad = jnp.stack(pieces, axis=1).astype(jnp.bfloat16)
    return (own_rows(outputs, rows)[None], own_rows(begins, rows)[None], weight_grad)


def solution(mesh):
    placed = (P("space", None, None), P("layer", None, None, None), P("space", None, None))
    return jax.shard_map(
        on_device,
        mesh=mesh,
        in_specs=placed,
        out_specs=(
            P("layer", "space", None, None),
            P("layer", "space", None, None),
            P("space", "layer", None, None),
        ),
        check_vma=False,
    )
```
